256 devices in a mesh: front: 32 (over y, x, core), row: 8 (over z).
Axes of the slice: x: 4, y: 4, z: 8, core: 2. Of those that a mesh axis runs over, the one named last changes fastest.
Arguments:
- rhs_front: bfloat16 [65536, 384], P(('front', 'row')), may hold values from -6 to 6
- rhs_root: float32 [12288, 384], P('row'), may hold values from -6 to 6
- pivot_inverse: bfloat16 [65536, 2048], P(('front', 'row')), may hold values from -0.125 to 0.125
- border_coupling: bfloat16 [196608, 2048], P(('front', 'row')), may hold values from -0.125 to 0.125
- root_inverse: bfloat16 [12288, 12288], P('front', 'row'), may hold values from -0.0546875 to 0.0546875
- border_map: int32 [32, 48], P('front', 'row'), may hold values from 0 to 95, as said below
Outputs:
- front_solution: float32 [65536, 384], P(('front', 'row'))
- root_solution: float32 [12288, 384], P(('front', 'row'))
The draws below stay inside these ranges and needn't reach their ends.
Inputs may be any that keep to these rules, and one draw needn't show every extreme that they name: `border_map`: for each front and each index r of row, the 6 border blocks held at that index name distinct root blocks, all among blocks r * 12 to (r + 1) * 12 - 1; a root block may be named by many fronts or by none.
All inputs are finite; a program needn't handle non-finite values.
Results may differ from the reference program's by a relative error of at most 0.0075.
Values may be sent and summed in bfloat16 or wider, within the bound.
A program may use at most 64 MiB of HBM per device.

```python
import jax
import jax.numpy as jnp
from jax import lax

PIV = 2048
BORD = 6144
ROOT = 12288
BLK = 128
NRHS = 384
FRONTS = 32
BORD_BLK = 6
SPAN_BLK = 12


def draw_border_map(key, part):
    span_blocks = SPAN_BLK
    per_device = BORD_BLK
    row_slices = BORD // BLK // BORD_BLK
    slice_count = FRONTS * row_slices
    jitter = jax.random.randint(jax.random.fold_in(key, 11), (slice_count, span_blocks), 0, 4096)
    favour = jax.random.randint(jax.random.fold_in(key, 12), (span_blocks,), 0, 3)
    favour = favour.at[0].set(3).at[span_blocks - 1].set(4)
    scores = (jitter + favour[None, :] * 1024) * span_blocks + jnp.arange(span_blocks, dtype=jnp.int32)[None, :]
    top_scores, chosen = lax.top_k(scores, per_device)
    offsets = jnp.arange(slice_count, dtype=jnp.int32) % row_slices * span_blocks
    return (chosen.astype(jnp.int32) + offsets[:, None]).reshape(FRONTS, per_device * row_slices)


def block_levels(key, dims, split, low, high):
    loudness = 1.0
    for dim, shards_of in split:
        steps = jax.random.uniform(jax.random.fold_in(jax.random.fold_in(key, 6), dim), (shards_of,), jnp.float32, low / len(split), high / len(split))
        loudness = loudness * jnp.repeat(jnp.exp(steps), dims[dim] // shards_of).reshape((-1,) + (1,) * (len(dims) - 1 - dim))
    return loudness


def noise(own_key, shape, width, limit, pieces=(), held_as=jnp.bfloat16):
    gain = block_levels(own_key, shape, pieces, -0.22, 0.18) if pieces else 1.0
    entries = jax.random.normal(own_key, shape, jnp.float32) * width * gain
    return jnp.minimum(jnp.maximum(entries, -limit), limit).astype(held_as)


def setup_inputs(seed: int = 0) -> dict:
    arg_keys = jax.random.split(jax.random.key(seed), 7)
    return {
        "rhs_front": noise(arg_keys[0], (FRONTS * PIV, NRHS), 1.0, 6.0, ((0, 256),)),
        "rhs_root": noise(arg_keys[1], (ROOT, NRHS), 1.0, 6.0, ((0, 8),), jnp.float32),
        "pivot_inverse": noise(arg_keys[2], (FRONTS * PIV, PIV), PIV ** -0.5, 0.125, ((0, 256),)),
        "border_coupling": noise(arg_keys[3], (FRONTS * BORD, PIV), PIV ** -0.5, 0.125, ((0, 256),)),
        "root_inverse": noise(arg_keys[4], (ROOT, ROOT), ROOT ** -0.5, 0.0546875, ((0, 32), (1, 8))),
        "border_map": draw_border_map(jax.random.fold_in(arg_keys[6], 71), 0),
    }


def reference(rhs_front, rhs_root, pivot_inverse, border_coupling, root_inverse, border_map):
    front_count = border_map.shape[0]
    block_count = BORD // BLK
    rhs_three = rhs_front.reshape(front_count, PIV, NRHS)
    pinv_three = pivot_inverse.reshape(front_count, PIV, PIV)
    coupling_three = border_coupling.reshape(front_count, BORD, PIV)

    def forward(items):
        pinv_one, coupling_one, rhs_one = items
        inner = jnp.dot(pinv_one, rhs_one, preferred_element_type=jnp.float32)
        contrib = jnp.dot(coupling_one, inner.astype(jnp.bfloat16), preferred_element_type=jnp.float32)
        return inner, contrib

    inner_all, contrib_all = lax.map(forward, (pinv_three, coupling_three, rhs_three))
    blocks = contrib_all.reshape(front_count * block_count, BLK * NRHS)
    assembled = jax.ops.segment_sum(blocks, border_map.reshape(-1), num_segments=ROOT // BLK)
    schur_rhs = (rhs_root - assembled.reshape(ROOT, NRHS)).astype(jnp.bfloat16)
    root_solution = jnp.dot(root_inverse, schur_rhs, preferred_element_type=jnp.float32)
    root_half = root_solution.astype(jnp.bfloat16)
    root_blocks = root_half.reshape(ROOT // BLK, BLK, NRHS)

    def backward(items):
        pinv_one, coupling_one, inner_one, index_row = items
        picked = jnp.take(root_blocks, index_row, axis=0).reshape(BORD, NRHS)
        pulled = lax.dot_general(coupling_one, picked, (((0,), (0,)), ((), ())), preferred_element_type=jnp.float32).astype(jnp.bfloat16)
        return inner_one - jnp.dot(pinv_one, pulled, preferred_element_type=jnp.float32)

    solved = lax.map(backward, (pinv_three, coupling_three, inner_all, border_map))
    return solved.reshape(front_count * PIV, NRHS), root_solution
```

```python
import functools

import jax
import jax.numpy as jnp
from jax import lax
from jax.experimental import pallas as pl
from jax.experimental.pallas import tpu as pltpu
from jax.sharding import PartitionSpec as P

BLK = 128
NX, NY, NZ = 4, 4, 8
PIECE = 48
CHUNKS = ((0, 128), (128, 128), (256, 128))
F32, BF16 = jnp.float32, jnp.bfloat16
N_COPIES = 80


def scratch_for(w):
    v = pltpu.VMEM
    return dict(
        g1=v((NZ, 256, w), BF16),
        inner=v((256, w), F32),
        g2=v((NZ, 256, w), BF16),
        contrib=v((6, BLK, w), F32),
        s0=v((6, BLK, w), F32),
        r0=v((6, BLK, w), F32),
        dense=v((768, w), F32),
        sx=v((2, 2, 192, w), F32),
        rx=v((2, 2, 192, w), F32),
        ey=v((192, w), F32),
        sy=v((2, 2, PIECE, w), F32),
        ry=v((2, 2, PIECE, w), F32),
        h=v((1536, w), BF16),
        part=v((384, w), F32),
        sz=v((2, 4, PIECE, w), F32),
        rz=v((2, 4, PIECE, w), F32),
        t=v((PIECE, w), BF16),
        k=v((1536, w), BF16),
        picked=v((768, w), BF16),
        q=v((NZ, w, 256), F32),
        sp=v((2, 4, w, 256), BF16),
        rp=v((2, 4, w, 256), BF16),
        g3=v((NZ, w, 256), BF16),
    )


NAMES = tuple(scratch_for(128))


def mod(a, n):
    return lax.rem(a + 2 * n, n)


def kernel(rhs, rroot, pinv, coup, rinv, bmap, out_f, out_r, *scratch):
    per = len(NAMES)
    bufs = [
        dict(zip(NAMES, scratch[i * per : (i + 1) * per])) for i in range(len(CHUNKS))
    ]
    pinv_v, coup_v, rinv_v, root_v, send_sems, recv_sems, load_sems = scratch[per * len(CHUNKS) :]

    f = lax.axis_index("front")
    z = lax.axis_index("row")
    c = lax.rem(f, 2)
    x = lax.rem(lax.div(f, 2), NX)
    y = lax.div(f, 2 * NX)

    def dev(x_, y_, c_, z_):
        return ((y_ * NX + x_) * 2 + c_, z_)

    rings = {
        "z": (NZ, z, dev(x, y, c, mod(z + 1, NZ)), dev(x, y, c, mod(z - 1, NZ))),
        "x": (NX, x, dev(mod(x + 1, NX), y, c, z), dev(mod(x - 1, NX), y, c, z)),
        "y": (NY, y, dev(x, mod(y + 1, NY), c, z), dev(x, mod(y - 1, NY), c, z)),
    }
    other = dev(x, y, 1 - c, z)
    perm_to = dev(
        mod(x + 2 * lax.div(z, 4), NX), mod(y + z, NY), 1 - c, 2 * y + lax.div(x, 2)
    )
    piece_out = (2 * lax.rem(x, 2) + c) * NZ + z
    y0 = lax.div(z, 2)
    x0 = 2 * lax.rem(z, 2)
    core_from = 1 - c

    def group_of(x_at):
        d = mod(x_at - x0, NX)
        return (2 * lax.rem(d, 2) + core_from) * NZ + 4 * lax.div(d, 2)

    def low_of(y_at):
        return mod(y_at - y0, NY)

    d_me = mod(x - x0, NX)
    perm_from = dev(
        x0 + lax.rem(d_me, 2), y0, core_from, 4 * lax.div(d_me, 2) + low_of(y)
    )

    loads = {}

    def load(name, src, dst):
        copy = pltpu.make_async_copy(src, dst, load_sems.at[len(loads)])
        copy.start()
        loads[name] = [copy, False]

    def need(name):
        entry = loads[name]
        if not entry[1]:
            entry[0].wait()
            entry[1] = True

    barrier = pltpu.get_barrier_semaphore()
    partners = [other, perm_to, perm_from]
    for _, _, plus, minus in rings.values():
        partners += [plus, minus]
    for partner in partners:
        pl.semaphore_signal(
            barrier, inc=1, device_id=partner, device_id_type=pl.DeviceIdType.MESH
        )
    piece_row = pl.multiple_of(((c * NX + x) * NY + y) * PIECE, 8)
    for i, (c0, w) in enumerate(CHUNKS):
        load(f"own{i}", rhs.at[:, pl.ds(c0, w)], bufs[i]["g1"].at[z])
    load("pinv", pinv, pinv_v)
    load("coup", coup, coup_v)
    load("root", rroot.at[pl.ds(piece_row, PIECE), :], root_v)
    load("rinv", rinv, rinv_v)
    pl.semaphore_wait(barrier, len(partners))

    starts = []

    def chunk(i, c0, w):
        b = bufs[i]
        count = [0]
        own_copies = []

        def send(src, dst, to):
            at = count[0]
            count[0] += 1
            copy = pltpu.make_async_remote_copy(
                src_ref=src,
                dst_ref=dst,
                send_sem=send_sems.at[i, at],
                recv_sem=recv_sems.at[i, at],
                device_id=to,
                device_id_type=pl.DeviceIdType.MESH,
            )
            copy.start()
            own_copies.append(copy)
            return copy

        def gather(axis, slot, split, first=None):
            n, me, plus, minus = rings[axis]
            half = n // 2
            src = slot(me) if first is None else first
            a = send(src, slot(me), plus)
            d = send(src, slot(me), minus)
            for s in range(1, half):
                yield
                a.wait_recv()
                got = slot(mod(me - s, n))
                if s == half - 1:
                    got = split(got, 0)
                a = send(got, got, plus)
                d.wait_recv()
                got = slot(mod(me + s, n))
                if s == half - 1:
                    got = split(got, 1)
                d = send(got, got, minus)
            yield
            a.wait_recv()
            d.wait_recv()

        def scatter(axis, own, rows, cut, sbuf, rbuf, wire):
            n, me, plus, minus = rings[axis]
            half = n // 2
            far = own(mod(me + half, n))
            sides = ((slice(0, cut), plus), (slice(cut, rows), minus))
            copies = []
            for side, (span, to) in enumerate(sides):
                sbuf[side, 0, span, :] = far[span, :].astype(wire)
                copies.append(
                    send(sbuf.at[side, 0, span, :], rbuf.at[side, 0, span, :], to)
                )
            for s in range(1, half):
                yield
                for side, (span, to) in enumerate(sides):
                    copies[side].wait_recv()
                    at = mod(me + half - s, n) if side == 0 else mod(me - half + s, n)
                    mine = own(at)
                    if s == 1:
                        rest = slice(cut, rows) if side == 0 else slice(0, cut)
                        sbuf[side, 1, span, :] = (
                            mine[span, :] + rbuf[side, 0, span, :].astype(F32)
                        ).astype(wire)
                        sbuf[side, 1, rest, :] = mine[rest, :].astype(wire)
                    else:
                        sbuf[side, s] = (mine[...] + rbuf[side, s - 1].astype(F32)).astype(wire)
                    copies[side] = send(sbuf.at[side, s], rbuf.at[side, s], to)
            yield
            copies[0].wait_recv()
            copies[1].wait_recv()
            if half == 1:
                raise ValueError
            return (
                own(me)[...]
                + rbuf[0, half - 1].astype(F32)
                + rbuf[1, half - 1].astype(F32)
            )

        def halves(cut, rows):
            def split(ref, side):
                return ref.at[pl.ds(0, cut), :] if side == 0 else ref.at[pl.ds(cut, rows - cut), :]

            return split

        def rows_of(ref, start, size):
            return ref.at[pl.ds(pl.multiple_of(start, 16), size), :]

        yield from gather(
            "z", lambda at: b["g1"].at[at], halves(128, 256), first=rhs.at[:, pl.ds(c0, w)]
        )
        need(f"own{i}")
        need("pinv")
        inner = jnp.dot(
            pinv_v[...], b["g1"][...].reshape(2048, w), preferred_element_type=F32
        )
        b["inner"][...] = inner
        b["g2"][z] = inner.astype(BF16)
        yield from gather("z", lambda at: b["g2"].at[at], halves(128, 256))
        need("coup")
        b["contrib"][...] = jnp.dot(
            coup_v[...], b["g2"][...].reshape(2048, w), preferred_element_type=F32
        ).reshape(6, BLK, w)
        local = [bmap[0, j] - z * 12 for j in range(6)]

        def placed(block):
            total = b["contrib"][0] * (local[0] == block).astype(F32)
            for j in range(1, 6):
                total = total + b["contrib"][j] * (local[j] == block).astype(F32)
            return total

        for j in range(6):
            b["s0"][j] = placed((1 - c) * 6 + j)
        swap = send(b["s0"], b["r0"], other)
        for j in range(6):
            b["dense"][j * BLK : (j + 1) * BLK, :] = placed(c * 6 + j)
        yield
        swap.wait_recv()
        b["dense"][...] = b["dense"][...] + b["r0"][...].reshape(768, w)
        b["ey"][...] = yield from scatter(
            "x",
            lambda at: rows_of(b["dense"], at * 192, 192),
            192,
            96,
            b["sx"],
            b["rx"],
            F32,
        )
        total = yield from scatter(
            "y", lambda at: rows_of(b["ey"], at * PIECE, PIECE), PIECE, 24, b["sy"], b["ry"], F32
        )
        need("root")
        h_at = (c * NX + x) * NY
        rows_of(b["h"], (h_at + y) * PIECE, PIECE)[...] = (
            root_v[:, c0 : c0 + w] - total
        ).astype(BF16)
        yield from gather(
            "y", lambda at: rows_of(b["h"], (h_at + at) * PIECE, PIECE), halves(32, PIECE)
        )
        yield from gather(
            "x", lambda at: rows_of(b["h"], (c * NX + at) * 192, 192), halves(96, 192)
        )
        mine = rows_of(b["h"], c * 768, 768)
        swap = send(mine, mine, other)
        yield
        swap.wait_recv()
        need("rinv")
        b["part"][...] = jnp.dot(rinv_v[...], b["h"][...], preferred_element_type=F32)
        root = yield from scatter(
            "z",
            lambda at: rows_of(b["part"], at * PIECE, PIECE),
            PIECE,
            24,
            b["sz"],
            b["rz"],
            F32,
        )
        out_r[:, c0 : c0 + w] = root
        b["t"][...] = root.astype(BF16)
        moved = send(b["t"], rows_of(b["k"], piece_out * PIECE, PIECE), perm_to)
        yield
        moved.wait_recv()
        k_at = group_of(x)
        yield from gather(
            "y",
            lambda at: rows_of(b["k"], (k_at + low_of(at)) * PIECE, PIECE),
            halves(32, PIECE),
        )
        yield from gather(
            "x", lambda at: rows_of(b["k"], group_of(at) * PIECE, 192), halves(96, 192)
        )
        swaps = []
        for g in range(2):
            mine = rows_of(b["k"], (g * 16 + core_from * 8) * PIECE, 8 * PIECE)
            swaps.append(send(mine, mine, other))
        yield
        for swap in swaps:
            swap.wait_recv()
        for j in range(6):
            total = b["k"][0:BLK, :] * (local[j] == 0).astype(F32).astype(BF16)
            for at in range(1, 12):
                mask = (local[j] == at).astype(F32).astype(BF16)
                total = total + b["k"][at * BLK : (at + 1) * BLK, :] * mask
            b["picked"][j * BLK : (j + 1) * BLK, :] = total
        pulled = lax.dot_general(
            b["picked"][...],
            coup_v[...],
            (((0,), (0,)), ((), ())),
            preferred_element_type=F32,
        )
        for at in range(NZ):
            b["q"][at] = pulled[:, at * 256 : (at + 1) * 256]
        total = yield from scatter(
            "z", lambda at: b["q"].at[at], w, w // 2, b["sp"], b["rp"], BF16
        )
        b["g3"][z] = total.astype(BF16)
        yield from gather("z", lambda at: b["g3"].at[at], halves(w // 2, w))
        result = b["inner"][...]
        for at in range(NZ):
            result = result - lax.dot_general(
                pinv_v[:, at * 256 : (at + 1) * 256],
                b["g3"][at],
                (((1,), (1,)), ((), ())),
                preferred_element_type=F32,
            )
        out_f[:, c0 : c0 + w] = result
        for copy in own_copies:
            copy.wait_send()

    live = [chunk(i, c0, w) for i, (c0, w) in enumerate(CHUNKS)]
    while live:
        for gen in list(live):
            try:
                next(gen)
            except StopIteration:
                live.remove(gen)


def per_device(*args):
    scratch = []
    for _, w in CHUNKS:
        scratch += list(scratch_for(w).values())
    scratch += [
        pltpu.VMEM((256, 2048), BF16),
        pltpu.VMEM((768, 2048), BF16),
        pltpu.VMEM((384, 1536), BF16),
        pltpu.VMEM((PIECE, 384), F32),
        pltpu.SemaphoreType.DMA((len(CHUNKS), N_COPIES)),
        pltpu.SemaphoreType.DMA((len(CHUNKS), N_COPIES)),
        pltpu.SemaphoreType.DMA((8,)),
    ]
    hbm = pl.BlockSpec(memory_space=pl.ANY)
    vmem = pl.BlockSpec(memory_space=pltpu.VMEM)
    return pl.pallas_call(
        kernel,
        out_shape=(
            jax.ShapeDtypeStruct((256, 384), F32),
            jax.ShapeDtypeStruct((PIECE, 384), F32),
        ),
        in_specs=[hbm] * 5 + [pl.BlockSpec(memory_space=pltpu.SMEM)],
        out_specs=(vmem, vmem),
        scratch_shapes=scratch,
        compiler_params=pltpu.CompilerParams(
            collective_id=0, has_side_effects=True, vmem_limit_bytes=60 * 2**20
        ),
        name="solve",
    )(*args)


def solution(mesh):
    in_specs = (
        P(("front", "row"), None),
        P("row", None),
        P(("front", "row"), None),
        P(("front", "row"), None),
        P("front", "row"),
        P("front", "row"),
    )
    out_specs = (P(("front", "row"), None), P(("front", "row"), None))
    return jax.shard_map(
        per_device, mesh=mesh, in_specs=in_specs, out_specs=out_specs, check_vma=False
    )
```

```python
import functools

import jax
import jax.numpy as jnp
from jax import lax
from jax.experimental import pallas as pl
from jax.experimental.pallas import tpu as pltpu
from jax.sharding import PartitionSpec as P

BLK = 128
NX, NY, NZ = 4, 4, 8
PIECE = 48
CHUNKS = ((0, 128), (128, 128), (256, 128))
F32, BF16 = jnp.float32, jnp.bfloat16
OFFSETS = sorted(
    ((dx, dy) for dx in range(NX) for dy in range(NY) if dx or dy),
    key=lambda o: -(min(o[0], NX - o[0]) + min(o[1], NY - o[1])),
)
N_COPIES = 112


def scratch_for(w):
    v = pltpu.VMEM
    return dict(
        g1=v((NZ, 256, w), BF16),
        inner=v((256, w), F32),
        g2=v((NZ, 256, w), BF16),
        contrib=v((6, BLK, w), F32),
        s0=v((6, BLK, w), F32),
        r0=v((6, BLK, w), F32),
        dense=v((768, w), F32),
        sxy=v((768, w), BF16),
        rxy=v((16, PIECE, w), BF16),
        h=v((1536, w), BF16),
        part=v((384, w), F32),
        parth=v((384, w), BF16),
        r5=v((NZ, PIECE, w), BF16),
        t=v((PIECE, w), BF16),
        k=v((1536, w), BF16),
        picked=v((768, w), BF16),
        q=v((NZ, w, 256), F32),
        sp=v((2, 4, w, 256), BF16),
        rp=v((2, 4, w, 256), BF16),
        g3=v((NZ, w, 256), BF16),
    )


NAMES = tuple(scratch_for(128))


def mod(a, n):
    return lax.rem(a + 2 * n, n)


def kernel(rhs, rroot, pinv, coup, rinv, bmap, out_f, out_r, *scratch):
    per = len(NAMES)
    bufs = [
        dict(zip(NAMES, scratch[i * per : (i + 1) * per])) for i in range(len(CHUNKS))
    ]
    pinv_v, coup_v, rinv_v, root_v, send_sems, recv_sems, load_sems, pass_sems = scratch[per * len(CHUNKS) :]

    f = lax.axis_index("front")
    z = lax.axis_index("row")
    c = lax.rem(f, 2)
    x = lax.rem(lax.div(f, 2), NX)
    y = lax.div(f, 2 * NX)

    def dev(x_, y_, c_, z_):
        return ((y_ * NX + x_) * 2 + c_, z_)

    rings = {
        "z": (NZ, z, dev(x, y, c, mod(z + 1, NZ)), dev(x, y, c, mod(z - 1, NZ))),
        "x": (NX, x, dev(mod(x + 1, NX), y, c, z), dev(mod(x - 1, NX), y, c, z)),
        "y": (NY, y, dev(x, mod(y + 1, NY), c, z), dev(x, mod(y - 1, NY), c, z)),
    }
    other = dev(x, y, 1 - c, z)
    perm_to = dev(
        mod(x + 2 * lax.div(z, 4), NX), mod(y + z, NY), 1 - c, 2 * y + lax.div(x, 2)
    )
    piece_out = (2 * lax.rem(x, 2) + c) * NZ + z
    y0 = lax.div(z, 2)
    x0 = 2 * lax.rem(z, 2)
    core_from = 1 - c

    def group_of(x_at):
        d = mod(x_at - x0, NX)
        return (2 * lax.rem(d, 2) + core_from) * NZ + 4 * lax.div(d, 2)

    def low_of(y_at):
        return mod(y_at - y0, NY)

    loads = {}

    def load(name, src, dst):
        copy = pltpu.make_async_copy(src, dst, load_sems.at[len(loads)])
        copy.start()
        loads[name] = [copy, False]

    def need(name):
        entry = loads[name]
        if not entry[1]:
            entry[0].wait()
            entry[1] = True

    barrier = pltpu.get_barrier_semaphore()
    partners = [other]
    for _, _, plus, minus in rings.values():
        partners += [plus, minus]
    for partner in partners:
        pl.semaphore_signal(
            barrier, inc=1, device_id=partner, device_id_type=pl.DeviceIdType.MESH
        )
    piece_row = pl.multiple_of(((c * NX + x) * NY + y) * PIECE, 8)
    for i, (c0, w) in enumerate(CHUNKS):
        load(f"own{i}", rhs.at[:, pl.ds(c0, w)], bufs[i]["g1"].at[z])
    load("pinv", pinv, pinv_v)
    load("coup", coup, coup_v)
    load("root", rroot.at[pl.ds(piece_row, PIECE), :], root_v)
    load("rinv", rinv, rinv_v)
    pl.semaphore_wait(barrier, len(partners))

    def passing():
        for r in range(3):
            for axis in "xy":
                for to in rings[axis][2:]:
                    pl.semaphore_signal(
                        pass_sems.at[r], inc=1, device_id=to, device_id_type=pl.DeviceIdType.MESH
                    )
            yield
            pl.semaphore_wait(pass_sems.at[r], 4)

    passes = passing()
    all_copies = []

    def in_plane():
        for _ in passes:
            pass

    def chunk(i, c0, w):
        b = bufs[i]
        count = [0]

        def send(src, dst, to):
            at = count[0]
            assert at < N_COPIES
            count[0] += 1
            copy = pltpu.make_async_remote_copy(
                src_ref=src,
                dst_ref=dst,
                send_sem=send_sems.at[i, at],
                recv_sem=recv_sems.at[i, at],
                device_id=to,
                device_id_type=pl.DeviceIdType.MESH,
            )
            copy.start()
            all_copies.append(copy)
            return copy

        def gather(axis, slot, split, first=None):
            n, me, plus, minus = rings[axis]
            half = n // 2
            src = slot(me) if first is None else first
            a = send(src, slot(me), plus)
            d = send(src, slot(me), minus)
            for s in range(1, half):
                yield
                a.wait_recv()
                got = slot(mod(me - s, n))
                if s == half - 1:
                    got = split(got, 0)
                a = send(got, got, plus)
                d.wait_recv()
                got = slot(mod(me + s, n))
                if s == half - 1:
                    got = split(got, 1)
                d = send(got, got, minus)
            yield
            a.wait_recv()
            d.wait_recv()

        def scatter(axis, own, rows, cut, sbuf, rbuf, wire):
            n, me, plus, minus = rings[axis]
            half = n // 2
            far = own(mod(me + half, n))
            sides = ((slice(0, cut), plus), (slice(cut, rows), minus))
            copies = []
            for side, (span, to) in enumerate(sides):
                sbuf[side, 0, span, :] = far[span, :].astype(wire)
                copies.append(
                    send(sbuf.at[side, 0, span, :], rbuf.at[side, 0, span, :], to)
                )
            for s in range(1, half):
                yield
                for side, (span, to) in enumerate(sides):
                    copies[side].wait_recv()
                    at = mod(me + half - s, n) if side == 0 else mod(me - half + s, n)
                    mine = own(at)
                    if s == 1:
                        rest = slice(cut, rows) if side == 0 else slice(0, cut)
                        sbuf[side, 1, span, :] = (
                            mine[span, :] + rbuf[side, 0, span, :].astype(F32)
                        ).astype(wire)
                        sbuf[side, 1, rest, :] = mine[rest, :].astype(wire)
                    else:
                        sbuf[side, s] = (mine[...] + rbuf[side, s - 1].astype(F32)).astype(wire)
                    copies[side] = send(sbuf.at[side, s], rbuf.at[side, s], to)
            yield
            copies[0].wait_recv()
            copies[1].wait_recv()
            if half == 1:
                raise ValueError
            return (
                own(me)[...]
                + rbuf[0, half - 1].astype(F32)
                + rbuf[1, half - 1].astype(F32)
            )

        def to_plane(src_of, dst_of):
            copies = []
            for dx, dy in OFFSETS:
                to = (mod(x + dx, NX), mod(y + dy, NY))
                copies.append(send(src_of(*to), dst_of(dx, dy), dev(*to, c, z)))
            return copies

        def halves(cut, rows):
            def split(ref, side):
                return ref.at[pl.ds(0, cut), :] if side == 0 else ref.at[pl.ds(cut, rows - cut), :]

            return split

        def rows_of(ref, start, size):
            return ref.at[pl.ds(pl.multiple_of(start, 16), size), :]

        yield from gather(
            "z", lambda at: b["g1"].at[at], halves(128, 256), first=rhs.at[:, pl.ds(c0, w)]
        )
        need(f"own{i}")
        need("pinv")
        inner = jnp.dot(
            pinv_v[...], b["g1"][...].reshape(2048, w), preferred_element_type=F32
        )
        b["inner"][...] = inner
        b["g2"][z] = inner.astype(BF16)
        yield from gather("z", lambda at: b["g2"].at[at], halves(128, 256))
        need("coup")
        b["contrib"][...] = jnp.dot(
            coup_v[...], b["g2"][...].reshape(2048, w), preferred_element_type=F32
        ).reshape(6, BLK, w)
        local = [bmap[0, j] - z * 12 for j in range(6)]

        def placed(block):
            total = b["contrib"][0] * (local[0] == block).astype(F32)
            for j in range(1, 6):
                total = total + b["contrib"][j] * (local[j] == block).astype(F32)
            return total

        for j in range(6):
            b["s0"][j] = placed((1 - c) * 6 + j)
        swap = send(b["s0"], b["r0"], other)
        for j in range(6):
            b["dense"][j * BLK : (j + 1) * BLK, :] = placed(c * 6 + j)
        yield
        swap.wait_recv()
        b["dense"][...] = b["dense"][...] + b["r0"][...].reshape(768, w)
        b["sxy"][...] = b["dense"][...].astype(BF16)
        in_plane()
        mine = (x * NY + y) * PIECE
        copies = to_plane(
            lambda x_, y_: rows_of(b["sxy"], (x_ * NY + y_) * PIECE, PIECE),
            lambda dx, dy: b["rxy"].at[dx * NY + dy],
        )
        yield
        total = rows_of(b["dense"], mine, PIECE)[...]
        for (dx, dy), copy in zip(OFFSETS, copies):
            copy.wait_recv()
            total = total + b["rxy"][dx * NY + dy].astype(F32)
        need("root")
        piece = rows_of(b["h"], c * 768 + mine, PIECE)
        piece[...] = (root_v[:, c0 : c0 + w] - total).astype(BF16)
        copies = to_plane(lambda x_, y_: piece, lambda dx, dy: piece)
        yield
        for copy in copies:
            copy.wait_recv()
        mine = rows_of(b["h"], c * 768, 768)
        swap = send(mine, mine, other)
        need("rinv")

        def root_half(core):
            cols = pl.ds(pl.multiple_of(core * 768, 256), 768)
            return jnp.dot(
                rinv_v[:, cols], rows_of(b["h"], core * 768, 768)[...], preferred_element_type=F32
            )

        b["part"][...] = root_half(c)
        yield
        swap.wait_recv()
        part = b["part"][...] + root_half(1 - c)
        b["part"][...] = part
        b["parth"][...] = part.astype(BF16)
        copies = []
        for s in (4, 3, 5, 2, 6, 1, 7):
            at = mod(z + s, NZ)
            copies.append(
                send(rows_of(b["parth"], at * PIECE, PIECE), b["r5"].at[s], dev(x, y, c, at))
            )
        yield
        total = rows_of(b["part"], z * PIECE, PIECE)[...]
        for copy in copies:
            copy.wait_recv()
        for s in range(1, NZ):
            total = total + b["r5"][s].astype(F32)
        out_r[:, c0 : c0 + w] = total
        b["t"][...] = total.astype(BF16)
        moved = send(b["t"], rows_of(b["k"], piece_out * PIECE, PIECE), perm_to)
        yield
        moved.wait_recv()
        piece = rows_of(b["k"], (group_of(x) + low_of(y)) * PIECE, PIECE)
        copies = to_plane(lambda x_, y_: piece, lambda dx, dy: piece)
        yield
        for copy in copies:
            copy.wait_recv()
        swaps = []
        for g in range(2):
            mine = rows_of(b["k"], (g * 16 + core_from * 8) * PIECE, 8 * PIECE)
            swaps.append(send(mine, mine, other))
        yield
        for swap in swaps:
            swap.wait_recv()
        for j in range(6):
            total = b["k"][0:BLK, :] * (local[j] == 0).astype(F32).astype(BF16)
            for at in range(1, 12):
                mask = (local[j] == at).astype(F32).astype(BF16)
                total = total + b["k"][at * BLK : (at + 1) * BLK, :] * mask
            b["picked"][j * BLK : (j + 1) * BLK, :] = total
        pulled = lax.dot_general(
            b["picked"][...],
            coup_v[...],
            (((0,), (0,)), ((), ())),
            preferred_element_type=F32,
        )
        for at in range(NZ):
            b["q"][at] = pulled[:, at * 256 : (at + 1) * 256]
        total = yield from scatter(
            "z", lambda at: b["q"].at[at], w, w // 2, b["sp"], b["rp"], BF16
        )
        b["g3"][z] = total.astype(BF16)
        yield from gather("z", lambda at: b["g3"].at[at], halves(w // 2, w))
        result = b["inner"][...]
        for at in range(NZ):
            result = result - lax.dot_general(
                pinv_v[:, at * 256 : (at + 1) * 256],
                b["g3"][at],
                (((1,), (1,)), ((), ())),
                preferred_element_type=F32,
            )
        out_f[:, c0 : c0 + w] = result

    live = [chunk(i, c0, w) for i, (c0, w) in enumerate(CHUNKS)]
    while live:
        for gen in list(live):
            try:
                next(gen)
            except StopIteration:
                live.remove(gen)
    for copy in all_copies:
        copy.wait_send()


def per_device(*args):
    scratch = []
    for _, w in CHUNKS:
        scratch += list(scratch_for(w).values())
    scratch += [
        pltpu.VMEM((256, 2048), BF16),
        pltpu.VMEM((768, 2048), BF16),
        pltpu.VMEM((384, 1536), BF16),
        pltpu.VMEM((PIECE, 384), F32),
        pltpu.SemaphoreType.DMA((len(CHUNKS), N_COPIES)),
        pltpu.SemaphoreType.DMA((len(CHUNKS), N_COPIES)),
        pltpu.SemaphoreType.DMA((8,)),
        pltpu.SemaphoreType.REGULAR((3,)),
    ]
    hbm = pl.BlockSpec(memory_space=pl.ANY)
    vmem = pl.BlockSpec(memory_space=pltpu.VMEM)
    return pl.pallas_call(
        kernel,
        out_shape=(
            jax.ShapeDtypeStruct((256, 384), F32),
            jax.ShapeDtypeStruct((PIECE, 384), F32),
        ),
        in_specs=[hbm] * 5 + [pl.BlockSpec(memory_space=pltpu.SMEM)],
        out_specs=(vmem, vmem),
        scratch_shapes=scratch,
        compiler_params=pltpu.CompilerParams(
            collective_id=0, has_side_effects=True, vmem_limit_bytes=60 * 2**20
        ),
        name="solve",
    )(*args)


def solution(mesh):
    in_specs = (
        P(("front", "row"), None),
        P("row", None),
        P(("front", "row"), None),
        P(("front", "row"), None),
        P("front", "row"),
        P("front", "row"),
    )
    out_specs = (P(("front", "row"), None), P(("front", "row"), None))
    return jax.shard_map(
        per_device, mesh=mesh, in_specs=in_specs, out_specs=out_specs, check_vma=False
    )
```

```python
import functools

import jax
import jax.numpy as jnp
from jax import lax
from jax.experimental import pallas as pl
from jax.experimental.pallas import tpu as pltpu
from jax.sharding import PartitionSpec as P

BLK = 128
NX, NY, NZ = 4, 4, 8
PIECE = 48
CHUNKS = ((0, 128), (128, 128), (256, 128))
F32, BF16 = jnp.float32, jnp.bfloat16
OFFSETS = sorted(
    ((dx, dy) for dx in range(NX) for dy in range(NY) if dx or dy),
    key=lambda o: -(min(o[0], NX - o[0]) + min(o[1], NY - o[1])),
)
N_SEMS = 28


def scratch_for(w):
    v = pltpu.VMEM
    return dict(
        g1=v((NZ, 256, w), BF16),
        inner=v((256, w), F32),
        g2=v((NZ, 256, w), BF16),
        contrib=v((6, BLK, w), F32),
        s0=v((6, BLK, w), BF16),
        r0=v((6, BLK, w), BF16),
        dense=v((768, w), F32),
        sxy=v((768, w), BF16),
        rxy=v((16, PIECE, w), BF16),
        h=v((1536, w), BF16),
        part=v((384, w), F32),
        parth=v((384, w), BF16),
        r5=v((NZ, PIECE, w), BF16),
        t=v((PIECE, w), BF16),
        k=v((1536, w), BF16),
        picked=v((768, w), BF16),
        q=v((NZ, w, 256), F32),
        sp=v((2, 4, w, 256), BF16),
        rp=v((2, 4, w, 256), BF16),
        g3=v((NZ, w, 256), BF16),
        rout=v((PIECE, w), F32),
        fout=v((256, w), F32),
    )


NAMES = tuple(scratch_for(128))


def mod(a, n):
    return lax.rem(a + 2 * n, n)


def kernel(rhs, rroot, pinv, coup, rinv, bmap, out_f, out_r, *scratch):
    per = len(NAMES)
    bufs = [
        dict(zip(NAMES, scratch[i * per : (i + 1) * per])) for i in range(len(CHUNKS))
    ]
    rhs_v, pinv_v, coup_v, rinv_v, root_v, sems, load_sems, store_sems, pass_sems = scratch[per * len(CHUNKS) :]

    f = lax.axis_index("front")
    z = lax.axis_index("row")
    c = lax.rem(f, 2)
    x = lax.rem(lax.div(f, 2), NX)
    y = lax.div(f, 2 * NX)

    def dev(x_, y_, c_, z_):
        return ((y_ * NX + x_) * 2 + c_, z_)

    rings = {
        "z": (NZ, z, dev(x, y, c, mod(z + 1, NZ)), dev(x, y, c, mod(z - 1, NZ))),
        "x": (NX, x, dev(mod(x + 1, NX), y, c, z), dev(mod(x - 1, NX), y, c, z)),
        "y": (NY, y, dev(x, mod(y + 1, NY), c, z), dev(x, mod(y - 1, NY), c, z)),
    }
    other = dev(x, y, 1 - c, z)
    plane_to = 2 * y + lax.div(x, 2)
    u = mod(z - plane_to, NZ)
    h = 1 - lax.div(lax.rem(u + 1, NZ), 4)
    q = lax.rem(12 - u - 2 * h, NY)
    perm_to = dev(
        mod(x + h * (2 * lax.rem(x, 2) - 1), NX), mod(y + q, NY), 1 - c, plane_to
    )
    piece_out = (2 * lax.rem(x, 2) + c) * NZ + z
    core_from = 1 - c
    d = mod(x - 2 * lax.rem(z, 2), NX)
    h_from = lax.div(d, 2)
    q_from = mod(y - lax.div(z, 2), NY)
    u_from = lax.rem(3 + 4 * h_from + lax.rem(5 + 2 * h_from - q_from, NY), NZ)
    piece_in = (2 * lax.rem(lax.div(d + 1, 2), 2) + core_from) * NZ + lax.rem(z + u_from, NZ)

    loads = {}

    def load(name, src, dst):
        copy = pltpu.make_async_copy(src, dst, load_sems.at[len(loads)])
        copy.start()
        loads[name] = [copy, False]

    def need(name):
        entry = loads[name]
        if not entry[1]:
            entry[0].wait()
            entry[1] = True

    barrier = pltpu.get_barrier_semaphore()
    partners = [other]
    for _, _, plus, minus in rings.values():
        partners += [plus, minus]
    for partner in partners:
        pl.semaphore_signal(
            barrier, inc=1, device_id=partner, device_id_type=pl.DeviceIdType.MESH
        )
    piece_row = pl.multiple_of(((c * NX + x) * NY + y) * PIECE, 8)
    load("rhs", rhs, rhs_v)
    load("pinv", pinv, pinv_v)
    load("coup", coup, coup_v)
    load("root", rroot.at[pl.ds(piece_row, PIECE), :], root_v)
    load("rinv", rinv, rinv_v)
    need("rhs")
    for i, (c0, w) in enumerate(CHUNKS):
        bufs[i]["g1"][z] = rhs_v[:, c0 : c0 + w]
    pl.semaphore_wait(barrier, len(partners))

    def passing():
        for r in range(3):
            for axis in "xy":
                for to in rings[axis][2:]:
                    pl.semaphore_signal(
                        pass_sems.at[r], inc=1, device_id=to, device_id_type=pl.DeviceIdType.MESH
                    )
            yield
            pl.semaphore_wait(pass_sems.at[r], 4)

    passes = passing()
    all_sent = []
    stores = []

    def store(src, dst):
        copy = pltpu.make_async_copy(src, dst, store_sems.at[len(stores)])
        copy.start()
        stores.append(copy)


    def in_plane():
        for _ in passes:
            pass

    def chunk(i, c0, w):
        b = bufs[i]
        count = [0]

        def sem():
            at = count[0]
            count[0] += 1
            assert at < N_SEMS
            return sems.at[i, at]

        ring_sems = [[sem() for _ in range(4)] for _ in range(2)]

        def send(src, dst, to, out, into):
            copy = pltpu.make_async_remote_copy(
                src_ref=src,
                dst_ref=dst,
                send_sem=out,
                recv_sem=into,
                device_id=to,
                device_id_type=pl.DeviceIdType.MESH,
            )
            copy.start()
            return copy

        def sent(out, ref):
            all_sent.append((out, ref))

        def arrive(into, ref):
            pltpu.make_async_copy(ref, ref, into).wait()

        def gather(axis, slot, split, seven):
            n, me, plus, minus = rings[axis]
            half = n // 2
            out = sem()
            sent(out, seven)
            ups, downs = ring_sems
            a = send(slot(me), slot(me), plus, out, ups[0])
            d = send(slot(me), slot(me), minus, out, downs[0])
            for s in range(1, half):
                yield
                a.wait_recv()
                got = slot(mod(me - s, n))
                if s == half - 1:
                    got = split(got, 0)
                a = send(got, got, plus, out, ups[s])
                d.wait_recv()
                got = slot(mod(me + s, n))
                if s == half - 1:
                    got = split(got, 1)
                d = send(got, got, minus, out, downs[s])
            yield
            a.wait_recv()
            d.wait_recv()

        def scatter(axis, own, rows, cut, sbuf, rbuf, wire, seven):
            n, me, plus, minus = rings[axis]
            half = n // 2
            far = own(mod(me + half, n))
            sides = ((slice(0, cut), plus), (slice(cut, rows), minus))
            copies = []
            out = sem()
            sent(out, seven)
            for side, (span, to) in enumerate(sides):
                sbuf[side, 0, span, :] = far[span, :].astype(wire)
                copies.append(
                    send(
                        sbuf.at[side, 0, span, :],
                        rbuf.at[side, 0, span, :],
                        to,
                        out,
                        ring_sems[side][0],
                    )
                )
            for s in range(1, half):
                yield
                for side, (span, to) in enumerate(sides):
                    copies[side].wait_recv()
                    at = mod(me + half - s, n) if side == 0 else mod(me - half + s, n)
                    mine = own(at)
                    if s == 1:
                        rest = slice(cut, rows) if side == 0 else slice(0, cut)
                        sbuf[side, 1, span, :] = (
                            mine[span, :] + rbuf[side, 0, span, :].astype(F32)
                        ).astype(wire)
                        sbuf[side, 1, rest, :] = mine[rest, :].astype(wire)
                    else:
                        sbuf[side, s] = (mine[...] + rbuf[side, s - 1].astype(F32)).astype(wire)
                    copies[side] = send(
                        sbuf.at[side, s], rbuf.at[side, s], to, out, ring_sems[side][s]
                    )
            yield
            copies[0].wait_recv()
            copies[1].wait_recv()
            return (
                own(me)[...]
                + rbuf[0, half - 1].astype(F32)
                + rbuf[1, half - 1].astype(F32)
            )

        def to_plane(src_of, dst_of, fifteen):
            out, into = sem(), sem()
            for dx, dy in OFFSETS:
                to = (mod(x + dx, NX), mod(y + dy, NY))
                send(src_of(*to), dst_of(dx, dy), dev(*to, c, z), out, into)
            sent(out, fifteen)
            yield
            arrive(into, fifteen)

        def halves(cut, rows):
            def split(ref, side):
                return ref.at[pl.ds(0, cut), :] if side == 0 else ref.at[pl.ds(cut, rows - cut), :]

            return split

        def rows_of(ref, start, size):
            return ref.at[pl.ds(pl.multiple_of(start, 16), size), :]

        yield from gather(
            "z", lambda at: b["g1"].at[at], halves(128, 256), b["g1"].at[0:7]
        )
        need("pinv")
        inner = jnp.dot(
            pinv_v[...], b["g1"][...].reshape(2048, w), preferred_element_type=F32
        )
        b["inner"][...] = inner
        b["g2"][z] = inner.astype(BF16)
        yield from gather(
            "z", lambda at: b["g2"].at[at], halves(128, 256), b["g2"].at[0:7]
        )
        need("coup")
        b["contrib"][...] = jnp.dot(
            coup_v[...], b["g2"][...].reshape(2048, w), preferred_element_type=F32
        ).reshape(6, BLK, w)
        local = [bmap[0, j] - z * 12 for j in range(6)]

        def placed(block):
            total = b["contrib"][0] * (local[0] == block).astype(F32)
            for j in range(1, 6):
                total = total + b["contrib"][j] * (local[j] == block).astype(F32)
            return total

        for j in range(6):
            b["s0"][j] = placed((1 - c) * 6 + j).astype(BF16)
        out = sem()
        swap = send(b["s0"], b["r0"], other, out, sem())
        sent(out, b["s0"])
        for j in range(6):
            b["dense"][j * BLK : (j + 1) * BLK, :] = placed(c * 6 + j)
        yield
        swap.wait_recv()
        b["dense"][...] = b["dense"][...] + b["r0"][...].reshape(768, w).astype(F32)
        b["sxy"][...] = b["dense"][...].astype(BF16)
        in_plane()
        mine = (x * NY + y) * PIECE
        yield from to_plane(
            lambda x_, y_: rows_of(b["sxy"], (x_ * NY + y_) * PIECE, PIECE),
            lambda dx, dy: b["rxy"].at[dx * NY + dy],
            b["rxy"].at[1:16],
        )
        total = rows_of(b["dense"], mine, PIECE)[...]
        for at in range(1, 16):
            total = total + b["rxy"][at].astype(F32)
        need("root")
        piece = rows_of(b["h"], c * 768 + mine, PIECE)
        piece[...] = (root_v[:, c0 : c0 + w] - total).astype(BF16)
        yield from to_plane(lambda x_, y_: piece, lambda dx, dy: piece, b["h"].at[0:720, :])
        mine = rows_of(b["h"], c * 768, 768)
        out = sem()
        swap = send(mine, mine, other, out, sem())
        sent(out, mine)
        need("rinv")

        def root_half(core):
            cols = pl.ds(pl.multiple_of(core * 768, 256), 768)
            return jnp.dot(
                rinv_v[:, cols], rows_of(b["h"], core * 768, 768)[...], preferred_element_type=F32
            )

        b["part"][...] = root_half(c)
        yield
        swap.wait_recv()
        part = b["part"][...] + root_half(1 - c)
        b["part"][...] = part
        b["parth"][...] = part.astype(BF16)
        out, into = sem(), sem()
        for s in (4, 3, 5, 2, 6, 1, 7):
            at = mod(z + s, NZ)
            src = rows_of(b["parth"], at * PIECE, PIECE)
            send(src, b["r5"].at[s], dev(x, y, c, at), out, into)
        sent(out, b["r5"].at[1:8])
        yield
        arrive(into, b["r5"].at[1:8])
        total = rows_of(b["part"], z * PIECE, PIECE)[...]
        for s in range(1, NZ):
            total = total + b["r5"][s].astype(F32)
        b["rout"][...] = total
        store(b["rout"], out_r.at[i])
        b["t"][...] = total.astype(BF16)
        out = sem()
        moved = send(b["t"], rows_of(b["k"], piece_out * PIECE, PIECE), perm_to, out, sem())
        sent(out, b["t"])
        yield
        moved.wait_recv()
        piece = rows_of(b["k"], piece_in * PIECE, PIECE)
        yield from to_plane(lambda x_, y_: piece, lambda dx, dy: piece, b["k"].at[0:720, :])
        out, into = sem(), sem()
        for g in range(2):
            mine = rows_of(b["k"], (g * 16 + core_from * 8) * PIECE, 8 * PIECE)
            send(mine, mine, other, out, into)
        sent(out, b["k"].at[0:768, :])
        yield
        arrive(into, b["k"].at[0:768, :])
        for j in range(6):
            total = b["k"][0:BLK, :] * (local[j] == 0).astype(F32).astype(BF16)
            for at in range(1, 12):
                mask = (local[j] == at).astype(F32).astype(BF16)
                total = total + b["k"][at * BLK : (at + 1) * BLK, :] * mask
            b["picked"][j * BLK : (j + 1) * BLK, :] = total
        pulled = lax.dot_general(
            b["picked"][...],
            coup_v[...],
            (((0,), (0,)), ((), ())),
            preferred_element_type=F32,
        )
        for at in range(NZ):
            b["q"][at] = pulled[:, at * 256 : (at + 1) * 256]
        total = yield from scatter(
            "z", lambda at: b["q"].at[at], w, w // 2, b["sp"], b["rp"], BF16, b["g3"].at[0:7]
        )
        b["g3"][z] = total.astype(BF16)
        yield from gather(
            "z", lambda at: b["g3"].at[at], halves(w // 2, w), b["g3"].at[0:7]
        )
        result = b["inner"][...]
        for at in range(NZ):
            result = result - lax.dot_general(
                pinv_v[:, at * 256 : (at + 1) * 256],
                b["g3"][at],
                (((1,), (1,)), ((), ())),
                preferred_element_type=F32,
            )
        b["fout"][...] = result
        store(b["fout"], out_f.at[i])

    live = [chunk(i, c0, w) for i, (c0, w) in enumerate(CHUNKS)] + [passes]
    while live:
        for gen in list(live):
            try:
                next(gen)
            except StopIteration:
                live.remove(gen)
    for out, ref in all_sent:
        pltpu.make_async_copy(ref, ref, out).wait()
    for copy in stores:
        copy.wait()


def join(f_ref, r_ref, out_f, out_r):
    for i, (c0, w) in enumerate(CHUNKS):
        out_f[:, c0 : c0 + w] = f_ref[i]
        out_r[:, c0 : c0 + w] = r_ref[i]


def per_device(*args):
    scratch = []
    for _, w in CHUNKS:
        scratch += list(scratch_for(w).values())
    scratch += [
        pltpu.VMEM((256, 384), BF16),
        pltpu.VMEM((256, 2048), BF16),
        pltpu.VMEM((768, 2048), BF16),
        pltpu.VMEM((384, 1536), BF16),
        pltpu.VMEM((PIECE, 384), F32),
        pltpu.SemaphoreType.DMA((len(CHUNKS), N_SEMS)),
        pltpu.SemaphoreType.DMA((8,)),
        pltpu.SemaphoreType.DMA((2 * len(CHUNKS),)),
        pltpu.SemaphoreType.REGULAR((3,)),
    ]
    hbm = pl.BlockSpec(memory_space=pl.ANY)
    vmem = pl.BlockSpec(memory_space=pltpu.VMEM)
    n, w = len(CHUNKS), CHUNKS[0][1]
    parts = pl.pallas_call(
        kernel,
        out_shape=(
            jax.ShapeDtypeStruct((n, 256, w), F32),
            jax.ShapeDtypeStruct((n, PIECE, w), F32),
        ),
        in_specs=[hbm] * 5 + [pl.BlockSpec(memory_space=pltpu.SMEM)],
        out_specs=(hbm, hbm),
        scratch_shapes=scratch,
        compiler_params=pltpu.CompilerParams(
            collective_id=0, has_side_effects=True, vmem_limit_bytes=60 * 2**20
        ),
        name="solve",
    )(*args)
    return pl.pallas_call(
        join,
        out_shape=(
            jax.ShapeDtypeStruct((256, 384), F32),
            jax.ShapeDtypeStruct((PIECE, 384), F32),
        ),
        in_specs=[vmem, vmem],
        out_specs=(vmem, vmem),
        name="join",
    )(*parts)


def solution(mesh):
    in_specs = (
        P(("front", "row"), None),
        P("row", None),
        P(("front", "row"), None),
        P(("front", "row"), None),
        P("front", "row"),
        P("front", "row"),
    )
    out_specs = (P(("front", "row"), None), P(("front", "row"), None))
    return jax.shard_map(
        per_device, mesh=mesh, in_specs=in_specs, out_specs=out_specs, check_vma=False
    )
```

```python
import functools

import jax
import jax.numpy as jnp
from jax import lax
from jax.experimental import pallas as pl
from jax.experimental.pallas import tpu as pltpu
from jax.sharding import PartitionSpec as P

BLK = 128
NX, NY, NZ = 4, 4, 8
PIECE = 48
CHUNKS = ((0, 128), (128, 128), (256, 128))
F32, BF16 = jnp.float32, jnp.bfloat16
OFFSETS = sorted(
    ((dx, dy) for dx in range(NX) for dy in range(NY) if dx or dy),
    key=lambda o: -(min(o[0], NX - o[0]) + min(o[1], NY - o[1])),
)
N_SEMS = 28
DELAYS = (0, 0, 1)


def scratch_for(w):
    v = pltpu.VMEM
    return dict(
        g1=v((NZ, 256, w), BF16),
        inner=v((256, w), F32),
        g2=v((NZ, 256, w), BF16),
        contrib=v((768, w), F32),
        s0=v((6, BLK, w), BF16),
        r0=v((6, BLK, w), BF16),
        dense=v((768, w), F32),
        sxy=v((768, w), BF16),
        rxy=v((16, PIECE, w), BF16),
        h=v((1536, w), BF16),
        part=v((384, w), F32),
        parth=v((384, w), BF16),
        r5=v((NZ, PIECE, w), BF16),
        t=v((PIECE, w), BF16),
        k=v((1536, w), BF16),
        picked=v((768, w), BF16),
        turned=v((w, 768), BF16),
        q=v((NZ, w, 256), F32),
        sp=v((2, 4, w, 256), BF16),
        rp=v((2, 4, w, 256), BF16),
        g3=v((NZ, w, 256), BF16),
    )


NAMES = tuple(scratch_for(128))


def mod(a, n):
    return lax.rem(a + 2 * n, n)


def kernel(rhs, rroot, pinv, coup, rinv, bmap, out_f, out_r, *scratch):
    per = len(NAMES)
    bufs = [
        dict(zip(NAMES, scratch[i * per : (i + 1) * per])) for i in range(len(CHUNKS))
    ]
    rhs_v, pinv_v, coup_v, rinv_v, root_v, sems, load_sems, pass_sems = scratch[per * len(CHUNKS) :]

    f = lax.axis_index("front")
    z = lax.axis_index("row")
    c = lax.rem(f, 2)
    x = lax.rem(lax.div(f, 2), NX)
    y = lax.div(f, 2 * NX)

    def dev(x_, y_, c_, z_):
        return ((y_ * NX + x_) * 2 + c_, z_)

    rings = {
        "z": (NZ, z, dev(x, y, c, mod(z + 1, NZ)), dev(x, y, c, mod(z - 1, NZ))),
        "x": (NX, x, dev(mod(x + 1, NX), y, c, z), dev(mod(x - 1, NX), y, c, z)),
        "y": (NY, y, dev(x, mod(y + 1, NY), c, z), dev(x, mod(y - 1, NY), c, z)),
    }
    other = dev(x, y, 1 - c, z)
    plane_to = 2 * y + lax.div(x, 2)
    u = mod(z - plane_to, NZ)
    h = 1 - lax.div(lax.rem(u + 1, NZ), 4)
    q = lax.rem(12 - u - 2 * h, NY)
    perm_to = dev(
        mod(x + h * (2 * lax.rem(x, 2) - 1), NX), mod(y + q, NY), 1 - c, plane_to
    )
    piece_out = (2 * lax.rem(x, 2) + c) * NZ + z
    core_from = 1 - c
    d = mod(x - 2 * lax.rem(z, 2), NX)
    h_from = lax.div(d, 2)
    q_from = mod(y - lax.div(z, 2), NY)
    u_from = lax.rem(3 + 4 * h_from + lax.rem(5 + 2 * h_from - q_from, NY), NZ)
    piece_in = (2 * lax.rem(lax.div(d + 1, 2), 2) + core_from) * NZ + lax.rem(z + u_from, NZ)

    loads = {}

    def load(name, src, dst):
        copy = pltpu.make_async_copy(src, dst, load_sems.at[len(loads)])
        copy.start()
        loads[name] = [copy, False]

    def need(name):
        entry = loads[name]
        if not entry[1]:
            entry[0].wait()
            entry[1] = True

    barrier = pltpu.get_barrier_semaphore()
    partners = [other]
    for _, _, plus, minus in rings.values():
        partners += [plus, minus]
    for partner in partners:
        pl.semaphore_signal(
            barrier, inc=1, device_id=partner, device_id_type=pl.DeviceIdType.MESH
        )
    piece_row = pl.multiple_of(((c * NX + x) * NY + y) * PIECE, 8)
    load("rhs", rhs, rhs_v)
    load("pinv", pinv, pinv_v)
    load("coup", coup, coup_v)
    load("root", rroot.at[pl.ds(piece_row, PIECE), :], root_v)
    load("rinv", rinv, rinv_v)
    need("rhs")
    for i, (c0, w) in enumerate(CHUNKS):
        bufs[i]["g1"][z] = rhs_v[:, c0 : c0 + w]
    pl.semaphore_wait(barrier, len(partners))

    def passing():
        for r in range(3):
            for axis in "xy":
                for to in rings[axis][2:]:
                    pl.semaphore_signal(
                        pass_sems.at[r], inc=1, device_id=to, device_id_type=pl.DeviceIdType.MESH
                    )
            yield
            pl.semaphore_wait(pass_sems.at[r], 4)

    passes = passing()
    all_sent = []
    def in_plane():
        for _ in passes:
            pass

    def chunk(i, c0, w):
        b = bufs[i]
        count = [0]

        def sem():
            at = count[0]
            count[0] += 1
            assert at < N_SEMS
            return sems.at[i, at]

        ring_sems = [[sem() for _ in range(4)] for _ in range(2)]

        def send(src, dst, to, out, into):
            copy = pltpu.make_async_remote_copy(
                src_ref=src,
                dst_ref=dst,
                send_sem=out,
                recv_sem=into,
                device_id=to,
                device_id_type=pl.DeviceIdType.MESH,
            )
            copy.start()
            return copy

        def sent(out, ref):
            all_sent.append((out, ref))

        def arrive(into, ref):
            pltpu.make_async_copy(ref, ref, into).wait()

        def gather(axis, slot, split, seven, seen):
            n, me, plus, minus = rings[axis]
            half = n // 2
            out = sem()
            sent(out, seven)
            ups, downs = ring_sems
            a = send(slot(me), slot(me), plus, out, ups[0])
            d = send(slot(me), slot(me), minus, out, downs[0])
            seen(me)
            for s in range(1, half):
                yield
                a.wait_recv()
                got = slot(mod(me - s, n))
                if s == half - 1:
                    got = split(got, 0)
                a = send(got, got, plus, out, ups[s])
                d.wait_recv()
                got = slot(mod(me + s, n))
                if s == half - 1:
                    got = split(got, 1)
                d = send(got, got, minus, out, downs[s])
                seen(mod(me - s, n))
                seen(mod(me + s, n))
            yield
            a.wait_recv()
            d.wait_recv()
            seen(mod(me + half, n))

        def scatter(axis, own, make, rows, cut, sbuf, rbuf, wire, seven):
            n, me, plus, minus = rings[axis]
            half = n // 2
            make(mod(me + half, n))
            far = own(mod(me + half, n))
            sides = ((slice(0, cut), plus), (slice(cut, rows), minus))
            copies = []
            out = sem()
            sent(out, seven)
            for side, (span, to) in enumerate(sides):
                sbuf[side, 0, span, :] = far[span, :].astype(wire)
                copies.append(
                    send(
                        sbuf.at[side, 0, span, :],
                        rbuf.at[side, 0, span, :],
                        to,
                        out,
                        ring_sems[side][0],
                    )
                )
            for s in range(1, half):
                make(mod(me + half - s, n))
                make(mod(me - half + s, n))
                yield
                for side, (span, to) in enumerate(sides):
                    copies[side].wait_recv()
                    at = mod(me + half - s, n) if side == 0 else mod(me - half + s, n)
                    mine = own(at)
                    if s == 1:
                        rest = slice(cut, rows) if side == 0 else slice(0, cut)
                        sbuf[side, 1, span, :] = (
                            mine[span, :] + rbuf[side, 0, span, :].astype(F32)
                        ).astype(wire)
                        sbuf[side, 1, rest, :] = mine[rest, :].astype(wire)
                    else:
                        sbuf[side, s] = (mine[...] + rbuf[side, s - 1].astype(F32)).astype(wire)
                    copies[side] = send(
                        sbuf.at[side, s], rbuf.at[side, s], to, out, ring_sems[side][s]
                    )
            make(me)
            yield
            copies[0].wait_recv()
            copies[1].wait_recv()
            return (
                own(me)[...]
                + rbuf[0, half - 1].astype(F32)
                + rbuf[1, half - 1].astype(F32)
            )

        def to_plane(src_of, dst_of, fifteen):
            out, into = sem(), sem()
            for dx, dy in OFFSETS:
                to = (mod(x + dx, NX), mod(y + dy, NY))
                send(src_of(*to), dst_of(dx, dy), dev(*to, c, z), out, into)
            sent(out, fifteen)
            yield
            arrive(into, fifteen)

        def halves(cut, rows):
            def split(ref, side):
                return ref.at[pl.ds(0, cut), :] if side == 0 else ref.at[pl.ds(cut, rows - cut), :]

            return split

        def rows_of(ref, start, size):
            return ref.at[pl.ds(pl.multiple_of(start, 16), size), :]

        def cols(ref, at):
            return ref[:, pl.ds(pl.multiple_of(at * 256, 256), 256)]

        def summing(acc, weights, pieces, name):
            first = [True]

            def seen(at):
                need(name)
                term = jnp.dot(cols(weights, at), pieces[at], preferred_element_type=F32)
                acc[...] = term if first[0] else acc[...] + term
                first[0] = False

            return seen

        yield from gather(
            "z", lambda at: b["g1"].at[at], halves(128, 256), b["g1"].at[0:7],
            summing(b["inner"], pinv_v, b["g1"], "pinv"),
        )
        b["g2"][z] = b["inner"][...].astype(BF16)
        yield from gather(
            "z", lambda at: b["g2"].at[at], halves(128, 256), b["g2"].at[0:7],
            summing(b["contrib"], coup_v, b["g2"], "coup"),
        )
        local = [bmap[0, j] - z * 12 for j in range(6)]

        def placed(block):
            total = b["contrib"][0:BLK, :] * (local[0] == block).astype(F32)
            for j in range(1, 6):
                total = total + b["contrib"][j * BLK : (j + 1) * BLK, :] * (local[j] == block).astype(F32)
            return total

        for j in range(6):
            b["s0"][j] = placed((1 - c) * 6 + j).astype(BF16)
        out = sem()
        swap = send(b["s0"], b["r0"], other, out, sem())
        sent(out, b["s0"])
        for j in range(6):
            b["dense"][j * BLK : (j + 1) * BLK, :] = placed(c * 6 + j)
        yield
        swap.wait_recv()
        b["dense"][...] = b["dense"][...] + b["r0"][...].reshape(768, w).astype(F32)
        b["sxy"][...] = b["dense"][...].astype(BF16)
        in_plane()
        mine = (x * NY + y) * PIECE
        yield from to_plane(
            lambda x_, y_: rows_of(b["sxy"], (x_ * NY + y_) * PIECE, PIECE),
            lambda dx, dy: b["rxy"].at[dx * NY + dy],
            b["rxy"].at[1:16],
        )
        total = rows_of(b["dense"], mine, PIECE)[...]
        for at in range(1, 16):
            total = total + b["rxy"][at].astype(F32)
        need("root")
        piece = rows_of(b["h"], c * 768 + mine, PIECE)
        piece[...] = (root_v[:, c0 : c0 + w] - total).astype(BF16)
        yield from to_plane(lambda x_, y_: piece, lambda dx, dy: piece, b["h"].at[0:720, :])
        mine = rows_of(b["h"], c * 768, 768)
        out = sem()
        swap = send(mine, mine, other, out, sem())
        sent(out, mine)
        need("rinv")

        def root_half(core):
            cols = pl.ds(pl.multiple_of(core * 768, 256), 768)
            return jnp.dot(
                rinv_v[:, cols], rows_of(b["h"], core * 768, 768)[...], preferred_element_type=F32
            )

        b["part"][...] = root_half(c)
        yield
        swap.wait_recv()
        part = b["part"][...] + root_half(1 - c)
        b["part"][...] = part
        b["parth"][...] = part.astype(BF16)
        out, into = sem(), sem()
        for s in (4, 3, 5, 2, 6, 1, 7):
            at = mod(z + s, NZ)
            src = rows_of(b["parth"], at * PIECE, PIECE)
            send(src, b["r5"].at[s], dev(x, y, c, at), out, into)
        sent(out, b["r5"].at[1:8])
        yield
        arrive(into, b["r5"].at[1:8])
        total = rows_of(b["part"], z * PIECE, PIECE)[...]
        for s in range(1, NZ):
            total = total + b["r5"][s].astype(F32)
        out_r[i] = total
        b["t"][...] = total.astype(BF16)
        out = sem()
        moved = send(b["t"], rows_of(b["k"], piece_out * PIECE, PIECE), perm_to, out, sem())
        sent(out, b["t"])
        yield
        moved.wait_recv()
        piece = rows_of(b["k"], piece_in * PIECE, PIECE)
        yield from to_plane(lambda x_, y_: piece, lambda dx, dy: piece, b["k"].at[0:720, :])
        out, into = sem(), sem()
        for g in range(2):
            mine = rows_of(b["k"], (g * 16 + core_from * 8) * PIECE, 8 * PIECE)
            send(mine, mine, other, out, into)
        sent(out, b["k"].at[0:768, :])
        yield
        arrive(into, b["k"].at[0:768, :])
        for j in range(6):
            total = b["k"][0:BLK, :] * (local[j] == 0).astype(F32).astype(BF16)
            for at in range(1, 12):
                mask = (local[j] == at).astype(F32).astype(BF16)
                total = total + b["k"][at * BLK : (at + 1) * BLK, :] * mask
            b["picked"][j * BLK : (j + 1) * BLK, :] = total
        b["turned"][...] = b["picked"][...].T

        def pull(at):
            b["q"][at] = jnp.dot(b["turned"][...], cols(coup_v, at), preferred_element_type=F32)

        total = yield from scatter(
            "z", lambda at: b["q"].at[at], pull, w, w // 2, b["sp"], b["rp"], BF16, b["g3"].at[0:7]
        )
        b["g3"][z] = total.astype(BF16)
        out_f_i = out_f.at[i]
        out_f_i[...] = b["inner"][...]

        def correct(at):
            out_f_i[...] = out_f_i[...] - lax.dot_general(
                cols(pinv_v, at),
                b["g3"][at],
                (((1,), (1,)), ((), ())),
                preferred_element_type=F32,
            )

        yield from gather(
            "z", lambda at: b["g3"].at[at], halves(w // 2, w), b["g3"].at[0:7], correct
        )

    live = [chunk(i, c0, w) for i, (c0, w) in enumerate(CHUNKS)] + [passes]
    wait = dict(zip(live, DELAYS))
    while live:
        for gen in list(live):
            if wait.get(gen, 0):
                wait[gen] -= 1
                continue
            try:
                next(gen)
            except StopIteration:
                live.remove(gen)
    for out, ref in all_sent:
        pltpu.make_async_copy(ref, ref, out).wait()


def join(f_ref, r_ref, out_f, out_r):
    for i, (c0, w) in enumerate(CHUNKS):
        out_f[:, c0 : c0 + w] = f_ref[i]
        out_r[:, c0 : c0 + w] = r_ref[i]


def per_device(*args):
    scratch = []
    for _, w in CHUNKS:
        scratch += list(scratch_for(w).values())
    scratch += [
        pltpu.VMEM((256, 384), BF16),
        pltpu.VMEM((256, 2048), BF16),
        pltpu.VMEM((768, 2048), BF16),
        pltpu.VMEM((384, 1536), BF16),
        pltpu.VMEM((PIECE, 384), F32),
        pltpu.SemaphoreType.DMA((len(CHUNKS), N_SEMS)),
        pltpu.SemaphoreType.DMA((8,)),
        pltpu.SemaphoreType.REGULAR((3,)),
    ]
    hbm = pl.BlockSpec(memory_space=pl.ANY)
    vmem = pl.BlockSpec(memory_space=pltpu.VMEM)
    n, w = len(CHUNKS), CHUNKS[0][1]
    parts = pl.pallas_call(
        kernel,
        out_shape=(
            pltpu.VMEM((n, 256, w), F32),
            pltpu.VMEM((n, PIECE, w), F32),
        ),
        in_specs=[hbm] * 5 + [pl.BlockSpec(memory_space=pltpu.SMEM)],
        out_specs=(vmem, vmem),
        scratch_shapes=scratch,
        compiler_params=pltpu.CompilerParams(
            collective_id=0, has_side_effects=True, vmem_limit_bytes=60 * 2**20
        ),
        name="solve",
    )(*args)
    return pl.pallas_call(
        join,
        out_shape=(
            jax.ShapeDtypeStruct((256, 384), F32),
            jax.ShapeDtypeStruct((PIECE, 384), F32),
        ),
        in_specs=[vmem, vmem],
        out_specs=(vmem, vmem),
        name="join",
    )(*[pltpu.with_memory_space_constraint(part, pltpu.VMEM) for part in parts])


def solution(mesh):
    in_specs = (
        P(("front", "row"), None),
        P("row", None),
        P(("front", "row"), None),
        P(("front", "row"), None),
        P("front", "row"),
        P("front", "row"),
    )
    out_specs = (P(("front", "row"), None), P(("front", "row"), None))
    return jax.shard_map(
        per_device, mesh=mesh, in_specs=in_specs, out_specs=out_specs, check_vma=False
    )
```

```python
import functools

import jax
import jax.numpy as jnp
from jax import lax
from jax.experimental import pallas as pl
from jax.experimental.pallas import tpu as pltpu
from jax.sharding import PartitionSpec as P

BLK = 128
NX, NY, NZ = 4, 4, 8
PIECE = 48
CHUNKS = ((0, 128), (128, 128), (256, 128))
F32, BF16 = jnp.float32, jnp.bfloat16
OFFSETS = sorted(
    ((dx, dy) for dx in range(NX) for dy in range(NY) if dx or dy),
    key=lambda o: -(min(o[0], NX - o[0]) + min(o[1], NY - o[1])),
)
N_SEMS = 28
DELAYS = (0, 0, 1)


def scratch_for(w):
    v = pltpu.VMEM
    return dict(
        g1=v((NZ, 256, w), BF16),
        inner=v((256, w), F32),
        g2=v((NZ, 256, w), BF16),
        contrib=v((768, w), F32),
        rounded=v((768, w), BF16),
        s0=v((6, BLK, w), BF16),
        r0=v((6, BLK, w), BF16),
        dense=v((768, w), F32),
        sxy=v((768, w), BF16),
        rxy=v((16, PIECE, w), BF16),
        h=v((1536, w), BF16),
        part=v((384, w), F32),
        parth=v((384, w), BF16),
        r5=v((NZ, PIECE, w), BF16),
        t=v((PIECE, w), BF16),
        k=v((1536, w), BF16),
        picked=v((768, w), BF16),
        turned=v((w, 768), BF16),
        q=v((NZ, w, 256), F32),
        sp=v((2, 4, w, 256), BF16),
        rp=v((2, 4, w, 256), BF16),
        g3=v((NZ, w, 256), BF16),
    )


NAMES = tuple(scratch_for(128))


def mod(a, n):
    return lax.rem(a + 2 * n, n)


def kernel(rhs, rroot, pinv, coup, rinv, bmap, out_f, out_r, *scratch):
    per = len(NAMES)
    bufs = [
        dict(zip(NAMES, scratch[i * per : (i + 1) * per])) for i in range(len(CHUNKS))
    ]
    rhs_v, pinv_v, coup_v, rinv_v, root_v, bmap_s, sems, load_sems, pass_sems = scratch[per * len(CHUNKS) :]

    f = lax.axis_index("front")
    z = lax.axis_index("row")
    c = lax.rem(f, 2)
    x = lax.rem(lax.div(f, 2), NX)
    y = lax.div(f, 2 * NX)

    def dev(x_, y_, c_, z_):
        return ((y_ * NX + x_) * 2 + c_, z_)

    rings = {
        "z": (NZ, z, dev(x, y, c, mod(z + 1, NZ)), dev(x, y, c, mod(z - 1, NZ))),
        "x": (NX, x, dev(mod(x + 1, NX), y, c, z), dev(mod(x - 1, NX), y, c, z)),
        "y": (NY, y, dev(x, mod(y + 1, NY), c, z), dev(x, mod(y - 1, NY), c, z)),
    }
    other = dev(x, y, 1 - c, z)
    plane_to = 2 * y + lax.div(x, 2)
    u = mod(z - plane_to, NZ)
    h = 1 - lax.div(lax.rem(u + 1, NZ), 4)
    q = lax.rem(12 - u - 2 * h, NY)
    perm_to = dev(
        mod(x + h * (2 * lax.rem(x, 2) - 1), NX), mod(y + q, NY), 1 - c, plane_to
    )
    piece_out = (2 * lax.rem(x, 2) + c) * NZ + z
    core_from = 1 - c
    d = mod(x - 2 * lax.rem(z, 2), NX)
    h_from = lax.div(d, 2)
    q_from = mod(y - lax.div(z, 2), NY)
    u_from = lax.rem(3 + 4 * h_from + lax.rem(5 + 2 * h_from - q_from, NY), NZ)
    piece_in = (2 * lax.rem(lax.div(d + 1, 2), 2) + core_from) * NZ + lax.rem(z + u_from, NZ)

    loads = {}

    def load(name, src, dst):
        copy = pltpu.make_async_copy(src, dst, load_sems.at[len(loads)])
        copy.start()
        loads[name] = [copy, False]

    def need(name):
        entry = loads[name]
        if not entry[1]:
            entry[0].wait()
            entry[1] = True

    barrier = pltpu.get_barrier_semaphore()
    partners = [other]
    for _, _, plus, minus in rings.values():
        partners += [plus, minus]
    for partner in partners:
        pl.semaphore_signal(
            barrier, inc=1, device_id=partner, device_id_type=pl.DeviceIdType.MESH
        )
    piece_row = pl.multiple_of(((c * NX + x) * NY + y) * PIECE, 8)
    load("rhs", rhs, rhs_v)
    load("pinv", pinv, pinv_v)
    load("coup", coup, coup_v)
    load("root", rroot.at[pl.ds(piece_row, PIECE), :], root_v)
    load("rinv", rinv, rinv_v)
    load("bmap", bmap, bmap_s)
    need("rhs")
    for i, (c0, w) in enumerate(CHUNKS):
        bufs[i]["g1"][z] = rhs_v[:, c0 : c0 + w]
    pl.semaphore_wait(barrier, len(partners))

    def passing():
        for r in range(3):
            for axis in "xy":
                for to in rings[axis][2:]:
                    pl.semaphore_signal(
                        pass_sems.at[r], inc=1, device_id=to, device_id_type=pl.DeviceIdType.MESH
                    )
            yield
            pl.semaphore_wait(pass_sems.at[r], 4)

    passes = passing()
    all_sent = []
    def in_plane():
        for _ in passes:
            pass

    def chunk(i, c0, w):
        b = bufs[i]
        count = [0]

        def sem():
            at = count[0]
            count[0] += 1
            assert at < N_SEMS
            return sems.at[i, at]

        ring_sems = [[sem() for _ in range(4)] for _ in range(2)]

        def send(src, dst, to, out, into):
            copy = pltpu.make_async_remote_copy(
                src_ref=src,
                dst_ref=dst,
                send_sem=out,
                recv_sem=into,
                device_id=to,
                device_id_type=pl.DeviceIdType.MESH,
            )
            copy.start()
            return copy

        def sent(out, ref):
            all_sent.append((out, ref))

        def arrive(into, ref):
            pltpu.make_async_copy(ref, ref, into).wait()

        def gather(axis, slot, split, seven, seen):
            n, me, plus, minus = rings[axis]
            half = n // 2
            out = sem()
            sent(out, seven)
            ups, downs = ring_sems
            a = send(slot(me), slot(me), plus, out, ups[0])
            d = send(slot(me), slot(me), minus, out, downs[0])
            pieces = [me]
            for s in range(1, half):
                yield
                for at in pieces:
                    seen(at)
                a.wait_recv()
                got = slot(mod(me - s, n))
                if s == half - 1:
                    got = split(got, 0)
                a = send(got, got, plus, out, ups[s])
                d.wait_recv()
                got = slot(mod(me + s, n))
                if s == half - 1:
                    got = split(got, 1)
                d = send(got, got, minus, out, downs[s])
                pieces = [mod(me - s, n), mod(me + s, n)]
            yield
            for at in pieces:
                seen(at)
            a.wait_recv()
            d.wait_recv()
            seen(mod(me + half, n))

        def scatter(axis, own, make, rows, cut, sbuf, rbuf, wire, seven):
            n, me, plus, minus = rings[axis]
            half = n // 2
            make(mod(me + half, n))
            far = own(mod(me + half, n))
            sides = ((slice(0, cut), plus), (slice(cut, rows), minus))
            copies = []
            out = sem()
            sent(out, seven)
            for side, (span, to) in enumerate(sides):
                sbuf[side, 0, span, :] = far[span, :].astype(wire)
                copies.append(
                    send(
                        sbuf.at[side, 0, span, :],
                        rbuf.at[side, 0, span, :],
                        to,
                        out,
                        ring_sems[side][0],
                    )
                )
            for s in range(1, half):
                yield
                make(mod(me + half - s, n))
                make(mod(me - half + s, n))
                for side, (span, to) in enumerate(sides):
                    copies[side].wait_recv()
                    at = mod(me + half - s, n) if side == 0 else mod(me - half + s, n)
                    mine = own(at)
                    if s == 1:
                        rest = slice(cut, rows) if side == 0 else slice(0, cut)
                        sbuf[side, 1, span, :] = (
                            mine[span, :] + rbuf[side, 0, span, :].astype(F32)
                        ).astype(wire)
                        sbuf[side, 1, rest, :] = mine[rest, :].astype(wire)
                    else:
                        sbuf[side, s] = (mine[...] + rbuf[side, s - 1].astype(F32)).astype(wire)
                    copies[side] = send(
                        sbuf.at[side, s], rbuf.at[side, s], to, out, ring_sems[side][s]
                    )
            yield
            make(me)
            copies[0].wait_recv()
            copies[1].wait_recv()
            return (
                own(me)[...]
                + rbuf[0, half - 1].astype(F32)
                + rbuf[1, half - 1].astype(F32)
            )

        def to_plane(src_of, dst_of, fifteen):
            out, into = sem(), sem()
            for dx, dy in OFFSETS:
                to = (mod(x + dx, NX), mod(y + dy, NY))
                send(src_of(*to), dst_of(dx, dy), dev(*to, c, z), out, into)
            sent(out, fifteen)
            yield
            arrive(into, fifteen)

        def halves(cut, rows):
            def split(ref, side):
                return ref.at[pl.ds(0, cut), :] if side == 0 else ref.at[pl.ds(cut, rows - cut), :]

            return split

        def rows_of(ref, start, size):
            return ref.at[pl.ds(pl.multiple_of(start, 16), size), :]

        def cols(ref, at):
            return ref[:, pl.ds(pl.multiple_of(at * 256, 256), 256)]

        def summing(acc, weights, pieces, name):
            first = [True]

            def seen(at):
                need(name)
                term = jnp.dot(cols(weights, at), pieces[at], preferred_element_type=F32)
                acc[...] = term if first[0] else acc[...] + term
                first[0] = False

            return seen

        yield from gather(
            "z", lambda at: b["g1"].at[at], halves(128, 256), b["g1"].at[0:7],
            summing(b["inner"], pinv_v, b["g1"], "pinv"),
        )
        b["g2"][z] = b["inner"][...].astype(BF16)
        yield from gather(
            "z", lambda at: b["g2"].at[at], halves(128, 256), b["g2"].at[0:7],
            summing(b["contrib"], coup_v, b["g2"], "coup"),
        )
        need("bmap")
        local = [bmap_s[0, j] - z * 12 for j in range(6)]

        def placed(block, name, kind):
            total = None
            for j in range(6):
                term = b[name][j * BLK : (j + 1) * BLK, :] * (local[j] == block).astype(F32).astype(kind)
                total = term if total is None else total + term
            return total

        b["rounded"][...] = b["contrib"][...].astype(BF16)

        for j in range(6):
            b["s0"][j] = placed((1 - c) * 6 + j, "rounded", BF16)
        out = sem()
        swap = send(b["s0"], b["r0"], other, out, sem())
        sent(out, b["s0"])
        for j in range(6):
            b["dense"][j * BLK : (j + 1) * BLK, :] = placed(c * 6 + j, "contrib", F32)
        yield
        swap.wait_recv()
        b["dense"][...] = b["dense"][...] + b["r0"][...].reshape(768, w).astype(F32)
        b["sxy"][...] = b["dense"][...].astype(BF16)
        in_plane()
        mine = (x * NY + y) * PIECE
        yield from to_plane(
            lambda x_, y_: rows_of(b["sxy"], (x_ * NY + y_) * PIECE, PIECE),
            lambda dx, dy: b["rxy"].at[dx * NY + dy],
            b["rxy"].at[1:16],
        )
        total = rows_of(b["dense"], mine, PIECE)[...]
        for at in range(1, 16):
            total = total + b["rxy"][at].astype(F32)
        need("root")
        piece = rows_of(b["h"], c * 768 + mine, PIECE)
        piece[...] = (root_v[:, c0 : c0 + w] - total).astype(BF16)
        yield from to_plane(lambda x_, y_: piece, lambda dx, dy: piece, b["h"].at[0:720, :])
        mine = rows_of(b["h"], c * 768, 768)
        out = sem()
        swap = send(mine, mine, other, out, sem())
        sent(out, mine)
        need("rinv")

        def root_half(core):
            cols = pl.ds(pl.multiple_of(core * 768, 256), 768)
            return jnp.dot(
                rinv_v[:, cols], rows_of(b["h"], core * 768, 768)[...], preferred_element_type=F32
            )

        b["part"][...] = root_half(c)
        yield
        swap.wait_recv()
        part = b["part"][...] + root_half(1 - c)
        b["part"][...] = part
        b["parth"][...] = part.astype(BF16)
        out, into = sem(), sem()
        for s in (4, 3, 5, 2, 6, 1, 7):
            at = mod(z + s, NZ)
            src = rows_of(b["parth"], at * PIECE, PIECE)
            send(src, b["r5"].at[s], dev(x, y, c, at), out, into)
        sent(out, b["r5"].at[1:8])
        yield
        arrive(into, b["r5"].at[1:8])
        total = rows_of(b["part"], z * PIECE, PIECE)[...]
        for s in range(1, NZ):
            total = total + b["r5"][s].astype(F32)
        out_r[i] = total
        b["t"][...] = total.astype(BF16)
        out = sem()
        moved = send(b["t"], rows_of(b["k"], piece_out * PIECE, PIECE), perm_to, out, sem())
        sent(out, b["t"])
        yield
        moved.wait_recv()
        piece = rows_of(b["k"], piece_in * PIECE, PIECE)
        yield from to_plane(lambda x_, y_: piece, lambda dx, dy: piece, b["k"].at[0:720, :])
        out, into = sem(), sem()
        for g in range(2):
            mine = rows_of(b["k"], (g * 16 + core_from * 8) * PIECE, 8 * PIECE)
            send(mine, mine, other, out, into)
        sent(out, b["k"].at[0:768, :])
        yield
        arrive(into, b["k"].at[0:768, :])
        for j in range(6):
            total = b["k"][0:BLK, :] * (local[j] == 0).astype(F32).astype(BF16)
            for at in range(1, 12):
                mask = (local[j] == at).astype(F32).astype(BF16)
                total = total + b["k"][at * BLK : (at + 1) * BLK, :] * mask
            b["picked"][j * BLK : (j + 1) * BLK, :] = total
        b["turned"][...] = b["picked"][...].T

        def pull(at):
            b["q"][at] = jnp.dot(b["turned"][...], cols(coup_v, at), preferred_element_type=F32)

        total = yield from scatter(
            "z", lambda at: b["q"].at[at], pull, w, w // 2, b["sp"], b["rp"], BF16, b["g3"].at[0:7]
        )
        b["g3"][z] = total.astype(BF16)
        out_f_i = out_f.at[i]
        out_f_i[...] = b["inner"][...]

        def correct(at):
            out_f_i[...] = out_f_i[...] - lax.dot_general(
                cols(pinv_v, at),
                b["g3"][at],
                (((1,), (1,)), ((), ())),
                preferred_element_type=F32,
            )

        yield from gather(
            "z", lambda at: b["g3"].at[at], halves(w // 2, w), b["g3"].at[0:7], correct
        )

    live = [chunk(i, c0, w) for i, (c0, w) in enumerate(CHUNKS)] + [passes]
    wait = dict(zip(live, DELAYS))
    while live:
        for gen in list(live):
            if wait.get(gen, 0):
                wait[gen] -= 1
                continue
            try:
                next(gen)
            except StopIteration:
                live.remove(gen)
    for out, ref in all_sent:
        pltpu.make_async_copy(ref, ref, out).wait()


def join(f_ref, r_ref, out_f, out_r):
    for i, (c0, w) in enumerate(CHUNKS):
        out_f[:, c0 : c0 + w] = f_ref[i]
        out_r[:, c0 : c0 + w] = r_ref[i]


def per_device(*args):
    scratch = []
    for _, w in CHUNKS:
        scratch += list(scratch_for(w).values())
    scratch += [
        pltpu.VMEM((256, 384), BF16),
        pltpu.VMEM((256, 2048), BF16),
        pltpu.VMEM((768, 2048), BF16),
        pltpu.VMEM((384, 1536), BF16),
        pltpu.VMEM((PIECE, 384), F32),
        pltpu.SMEM((1, 6), jnp.int32),
        pltpu.SemaphoreType.DMA((len(CHUNKS), N_SEMS)),
        pltpu.SemaphoreType.DMA((8,)),
        pltpu.SemaphoreType.REGULAR((3,)),
    ]
    hbm = pl.BlockSpec(memory_space=pl.ANY)
    vmem = pl.BlockSpec(memory_space=pltpu.VMEM)
    n, w = len(CHUNKS), CHUNKS[0][1]
    parts = pl.pallas_call(
        kernel,
        out_shape=(
            pltpu.VMEM((n, 256, w), F32),
            pltpu.VMEM((n, PIECE, w), F32),
        ),
        in_specs=[hbm] * 6,
        out_specs=(vmem, vmem),
        scratch_shapes=scratch,
        compiler_params=pltpu.CompilerParams(
            collective_id=0, has_side_effects=True, vmem_limit_bytes=60 * 2**20
        ),
        name="solve",
    )(*args)
    return pl.pallas_call(
        join,
        out_shape=(
            jax.ShapeDtypeStruct((256, 384), F32),
            jax.ShapeDtypeStruct((PIECE, 384), F32),
        ),
        in_specs=[vmem, vmem],
        out_specs=(vmem, vmem),
        name="join",
    )(*[pltpu.with_memory_space_constraint(part, pltpu.VMEM) for part in parts])


def solution(mesh):
    in_specs = (
        P(("front", "row"), None),
        P("row", None),
        P(("front", "row"), None),
        P(("front", "row"), None),
        P("front", "row"),
        P("front", "row"),
    )
    out_specs = (P(("front", "row"), None), P(("front", "row"), None))
    return jax.shard_map(
        per_device, mesh=mesh, in_specs=in_specs, out_specs=out_specs, check_vma=False
    )
```

```python
import functools

import jax
import jax.numpy as jnp
from jax import lax
from jax.experimental import pallas as pl
from jax.experimental.pallas import tpu as pltpu
from jax.sharding import PartitionSpec as P

BLK = 128
NX, NY, NZ = 4, 4, 8
PIECE = 48
CHUNKS = ((0, 128), (128, 128), (256, 128))
F32, BF16 = jnp.float32, jnp.bfloat16
OFFSETS = sorted(
    ((dx, dy) for dx in range(NX) for dy in range(NY) if dx or dy),
    key=lambda o: -(min(o[0], NX - o[0]) + min(o[1], NY - o[1])),
)
N_SEMS = 28
DELAYS = (0, 0, 1)


def scratch_for(w):
    v = pltpu.VMEM
    return dict(
        g1=v((NZ, 256, w), BF16),
        inner=v((256, w), F32),
        g2=v((NZ, 256, w), BF16),
        contrib=v((768, w), F32),
        rounded=v((768, w), BF16),
        s0=v((6, BLK, w), BF16),
        r0=v((6, BLK, w), BF16),
        dense=v((768, w), F32),
        sxy=v((768, w), BF16),
        rxy=v((16, PIECE, w), BF16),
        h=v((1536, w), BF16),
        part=v((384, w), F32),
        parth=v((384, w), BF16),
        r5=v((NZ, PIECE, w), BF16),
        t=v((PIECE, w), BF16),
        k=v((1536, w), BF16),
        picked=v((768, w), BF16),
        turned=v((w, 768), BF16),
        q=v((NZ, w, 256), F32),
        sp=v((2, 4, w, 256), BF16),
        rp=v((2, 4, w, 256), BF16),
        g3=v((NZ, w, 256), BF16),
    )


NAMES = tuple(scratch_for(128))


def mod(a, n):
    return lax.rem(a + 2 * n, n)


def kernel(rhs, rroot, pinv, coup, rinv, bmap, out_f, out_r, *scratch):
    per = len(NAMES)
    bufs = [
        dict(zip(NAMES, scratch[i * per : (i + 1) * per])) for i in range(len(CHUNKS))
    ]
    rhs_v, pinv_v, coup_v, rinv_v, root_v, bmap_s, sems, load_sems, pass_sems = scratch[per * len(CHUNKS) :]

    f = lax.axis_index("front")
    z = lax.axis_index("row")
    c = lax.rem(f, 2)
    x = lax.rem(lax.div(f, 2), NX)
    y = lax.div(f, 2 * NX)

    def dev(x_, y_, c_, z_):
        return ((y_ * NX + x_) * 2 + c_, z_)

    rings = {
        "z": (NZ, z, dev(x, y, c, mod(z + 1, NZ)), dev(x, y, c, mod(z - 1, NZ))),
        "x": (NX, x, dev(mod(x + 1, NX), y, c, z), dev(mod(x - 1, NX), y, c, z)),
        "y": (NY, y, dev(x, mod(y + 1, NY), c, z), dev(x, mod(y - 1, NY), c, z)),
    }
    other = dev(x, y, 1 - c, z)
    plane_to = 2 * y + lax.div(x, 2)
    u = mod(z - plane_to, NZ)
    h = 1 - lax.div(lax.rem(u + 1, NZ), 4)
    q = lax.rem(12 - u - 2 * h, NY)
    perm_to = dev(
        mod(x + h * (2 * lax.rem(x, 2) - 1), NX), mod(y + q, NY), 1 - c, plane_to
    )
    piece_out = (2 * lax.rem(x, 2) + c) * NZ + z
    core_from = 1 - c
    d = mod(x - 2 * lax.rem(z, 2), NX)
    h_from = lax.div(d, 2)
    q_from = mod(y - lax.div(z, 2), NY)
    u_from = lax.rem(3 + 4 * h_from + lax.rem(5 + 2 * h_from - q_from, NY), NZ)
    piece_in = (2 * lax.rem(lax.div(d + 1, 2), 2) + core_from) * NZ + lax.rem(z + u_from, NZ)

    loads = {}

    def load(name, src, dst):
        copy = pltpu.make_async_copy(src, dst, load_sems.at[len(loads)])
        copy.start()
        loads[name] = [copy, False]

    def need(name):
        entry = loads[name]
        if not entry[1]:
            entry[0].wait()
            entry[1] = True

    barrier = pltpu.get_barrier_semaphore()
    partners = [other]
    for _, _, plus, minus in rings.values():
        partners += [plus, minus]
    for partner in partners:
        pl.semaphore_signal(
            barrier, inc=1, device_id=partner, device_id_type=pl.DeviceIdType.MESH
        )
    piece_row = pl.multiple_of(((c * NX + x) * NY + y) * PIECE, 8)
    load("rhs", rhs, rhs_v)
    load("pinv", pinv, pinv_v)
    load("coup", coup, coup_v)
    load("root", rroot.at[pl.ds(piece_row, PIECE), :], root_v)
    load("rinv", rinv, rinv_v)
    load("bmap", bmap, bmap_s)
    need("rhs")
    pl.semaphore_wait(barrier, len(partners))

    def passing():
        for r in range(3):
            for axis in "xy":
                for to in rings[axis][2:]:
                    pl.semaphore_signal(
                        pass_sems.at[r], inc=1, device_id=to, device_id_type=pl.DeviceIdType.MESH
                    )
            yield
            pl.semaphore_wait(pass_sems.at[r], 4)

    passes = passing()
    all_sent = []
    def in_plane():
        for _ in passes:
            pass

    def chunk(i, c0, w):
        b = bufs[i]
        count = [0]

        def sem():
            at = count[0]
            count[0] += 1
            assert at < N_SEMS
            return sems.at[i, at]

        ring_sems = [[sem() for _ in range(4)] for _ in range(2)]

        def send(src, dst, to, out, into):
            copy = pltpu.make_async_remote_copy(
                src_ref=src,
                dst_ref=dst,
                send_sem=out,
                recv_sem=into,
                device_id=to,
                device_id_type=pl.DeviceIdType.MESH,
            )
            copy.start()
            return copy

        def sent(out, ref):
            all_sent.append((out, ref))

        def arrive(into, ref):
            pltpu.make_async_copy(ref, ref, into).wait()

        def gather(axis, slot, split, seven, seen):
            n, me, plus, minus = rings[axis]
            half = n // 2
            out = sem()
            sent(out, seven)
            ups, downs = ring_sems
            a = send(slot(me), slot(me), plus, out, ups[0])
            d = send(slot(me), slot(me), minus, out, downs[0])
            pieces = [me]
            for s in range(1, half):
                yield
                for at in pieces:
                    seen(at)
                a.wait_recv()
                got = slot(mod(me - s, n))
                if s == half - 1:
                    got = split(got, 0)
                a = send(got, got, plus, out, ups[s])
                d.wait_recv()
                got = slot(mod(me + s, n))
                if s == half - 1:
                    got = split(got, 1)
                d = send(got, got, minus, out, downs[s])
                pieces = [mod(me - s, n), mod(me + s, n)]
            yield
            for at in pieces:
                seen(at)
            a.wait_recv()
            d.wait_recv()
            seen(mod(me + half, n))

        def scatter(axis, own, make, rows, cut, sbuf, rbuf, wire, seven):
            n, me, plus, minus = rings[axis]
            half = n // 2
            make(mod(me + half, n))
            far = own(mod(me + half, n))
            sides = ((slice(0, cut), plus), (slice(cut, rows), minus))
            copies = []
            out = sem()
            sent(out, seven)
            for side, (span, to) in enumerate(sides):
                sbuf[side, 0, span, :] = far[span, :].astype(wire)
                copies.append(
                    send(
                        sbuf.at[side, 0, span, :],
                        rbuf.at[side, 0, span, :],
                        to,
                        out,
                        ring_sems[side][0],
                    )
                )
            for s in range(1, half):
                yield
                make(mod(me + half - s, n))
                make(mod(me - half + s, n))
                for side, (span, to) in enumerate(sides):
                    copies[side].wait_recv()
                    at = mod(me + half - s, n) if side == 0 else mod(me - half + s, n)
                    mine = own(at)
                    if s == 1:
                        rest = slice(cut, rows) if side == 0 else slice(0, cut)
                        sbuf[side, 1, span, :] = (
                            mine[span, :] + rbuf[side, 0, span, :].astype(F32)
                        ).astype(wire)
                        sbuf[side, 1, rest, :] = mine[rest, :].astype(wire)
                    else:
                        sbuf[side, s] = (mine[...] + rbuf[side, s - 1].astype(F32)).astype(wire)
                    copies[side] = send(
                        sbuf.at[side, s], rbuf.at[side, s], to, out, ring_sems[side][s]
                    )
            yield
            make(me)
            copies[0].wait_recv()
            copies[1].wait_recv()
            return (
                own(me)[...]
                + rbuf[0, half - 1].astype(F32)
                + rbuf[1, half - 1].astype(F32)
            )

        def to_plane(src_of, dst_of, fifteen):
            out, into = sem(), sem()
            for dx, dy in OFFSETS:
                to = (mod(x + dx, NX), mod(y + dy, NY))
                send(src_of(*to), dst_of(dx, dy), dev(*to, c, z), out, into)
            sent(out, fifteen)
            yield
            arrive(into, fifteen)

        def halves(cut, rows):
            def split(ref, side):
                return ref.at[pl.ds(0, cut), :] if side == 0 else ref.at[pl.ds(cut, rows - cut), :]

            return split

        def rows_of(ref, start, size):
            return ref.at[pl.ds(pl.multiple_of(start, 16), size), :]

        b["g1"][z] = rhs_v[:, c0 : c0 + w]

        def cols(ref, at):
            return ref[:, pl.ds(pl.multiple_of(at * 256, 256), 256)]

        def summing(acc, weights, pieces, name):
            first = [True]

            def seen(at):
                need(name)
                term = jnp.dot(cols(weights, at), pieces[at], preferred_element_type=F32)
                acc[...] = term if first[0] else acc[...] + term
                first[0] = False

            return seen

        yield from gather(
            "z", lambda at: b["g1"].at[at], halves(128, 256), b["g1"].at[0:7],
            summing(b["inner"], pinv_v, b["g1"], "pinv"),
        )
        b["g2"][z] = b["inner"][...].astype(BF16)
        yield from gather(
            "z", lambda at: b["g2"].at[at], halves(128, 256), b["g2"].at[0:7],
            summing(b["contrib"], coup_v, b["g2"], "coup"),
        )
        need("bmap")
        local = [bmap_s[0, j] - z * 12 for j in range(6)]

        def placed(block, name, kind):
            total = None
            for j in range(6):
                term = b[name][j * BLK : (j + 1) * BLK, :] * (local[j] == block).astype(F32).astype(kind)
                total = term if total is None else total + term
            return total

        b["rounded"][...] = b["contrib"][...].astype(BF16)

        for j in range(6):
            b["s0"][j] = placed((1 - c) * 6 + j, "rounded", BF16)
        out = sem()
        swap = send(b["s0"], b["r0"], other, out, sem())
        sent(out, b["s0"])
        for j in range(6):
            b["dense"][j * BLK : (j + 1) * BLK, :] = placed(c * 6 + j, "contrib", F32)
        yield
        swap.wait_recv()
        b["dense"][...] = b["dense"][...] + b["r0"][...].reshape(768, w).astype(F32)
        b["sxy"][...] = b["dense"][...].astype(BF16)
        in_plane()
        mine = (x * NY + y) * PIECE
        yield from to_plane(
            lambda x_, y_: rows_of(b["sxy"], (x_ * NY + y_) * PIECE, PIECE),
            lambda dx, dy: b["rxy"].at[dx * NY + dy],
            b["rxy"].at[1:16],
        )
        total = rows_of(b["dense"], mine, PIECE)[...]
        for at in range(1, 16):
            total = total + b["rxy"][at].astype(F32)
        need("root")
        piece = rows_of(b["h"], c * 768 + mine, PIECE)
        piece[...] = (root_v[:, c0 : c0 + w] - total).astype(BF16)
        yield from to_plane(lambda x_, y_: piece, lambda dx, dy: piece, b["h"].at[0:720, :])
        mine = rows_of(b["h"], c * 768, 768)
        out = sem()
        swap = send(mine, mine, other, out, sem())
        sent(out, mine)
        need("rinv")

        def root_half(core):
            cols = pl.ds(pl.multiple_of(core * 768, 256), 768)
            return jnp.dot(
                rinv_v[:, cols], rows_of(b["h"], core * 768, 768)[...], preferred_element_type=F32
            )

        b["part"][...] = root_half(c)
        yield
        swap.wait_recv()
        part = b["part"][...] + root_half(1 - c)
        b["part"][...] = part
        b["parth"][...] = part.astype(BF16)
        out, into = sem(), sem()
        for s in (4, 3, 5, 2, 6, 1, 7):
            at = mod(z + s, NZ)
            src = rows_of(b["parth"], at * PIECE, PIECE)
            send(src, b["r5"].at[s], dev(x, y, c, at), out, into)
        sent(out, b["r5"].at[1:8])
        yield
        arrive(into, b["r5"].at[1:8])
        total = rows_of(b["part"], z * PIECE, PIECE)[...]
        for s in range(1, NZ):
            total = total + b["r5"][s].astype(F32)
        out_r[i] = total
        b["t"][...] = total.astype(BF16)
        out = sem()
        moved = send(b["t"], rows_of(b["k"], piece_out * PIECE, PIECE), perm_to, out, sem())
        sent(out, b["t"])
        yield
        moved.wait_recv()
        piece = rows_of(b["k"], piece_in * PIECE, PIECE)
        yield from to_plane(lambda x_, y_: piece, lambda dx, dy: piece, b["k"].at[0:720, :])
        out, into = sem(), sem()
        for g in range(2):
            mine = rows_of(b["k"], (g * 16 + core_from * 8) * PIECE, 8 * PIECE)
            send(mine, mine, other, out, into)
        sent(out, b["k"].at[0:768, :])
        yield
        arrive(into, b["k"].at[0:768, :])
        for j in range(6):
            total = b["k"][0:BLK, :] * (local[j] == 0).astype(F32).astype(BF16)
            for at in range(1, 12):
                mask = (local[j] == at).astype(F32).astype(BF16)
                total = total + b["k"][at * BLK : (at + 1) * BLK, :] * mask
            b["picked"][j * BLK : (j + 1) * BLK, :] = total
        b["turned"][...] = b["picked"][...].T

        def pull(at):
            b["q"][at] = jnp.dot(b["turned"][...], cols(coup_v, at), preferred_element_type=F32)

        total = yield from scatter(
            "z", lambda at: b["q"].at[at], pull, w, w // 2, b["sp"], b["rp"], BF16, b["g3"].at[0:7]
        )
        b["g3"][z] = total.astype(BF16)
        out_f_i = out_f.at[i]
        out_f_i[...] = b["inner"][...]

        def correct(at):
            out_f_i[...] = out_f_i[...] - lax.dot_general(
                cols(pinv_v, at),
                b["g3"][at],
                (((1,), (1,)), ((), ())),
                preferred_element_type=F32,
            )

        yield from gather(
            "z", lambda at: b["g3"].at[at], halves(w // 2, w), b["g3"].at[0:7], correct
        )

    live = [chunk(i, c0, w) for i, (c0, w) in enumerate(CHUNKS)] + [passes]
    wait = dict(zip(live, DELAYS))
    while live:
        for gen in list(live):
            if wait.get(gen, 0):
                wait[gen] -= 1
                continue
            try:
                next(gen)
            except StopIteration:
                live.remove(gen)
    for out, ref in all_sent:
        pltpu.make_async_copy(ref, ref, out).wait()


def join(f_ref, r_ref, out_f, out_r):
    for i, (c0, w) in enumerate(CHUNKS):
        out_f[:, c0 : c0 + w] = f_ref[i]
        out_r[:, c0 : c0 + w] = r_ref[i]


def per_device(*args):
    scratch = []
    for _, w in CHUNKS:
        scratch += list(scratch_for(w).values())
    scratch += [
        pltpu.VMEM((256, 384), BF16),
        pltpu.VMEM((256, 2048), BF16),
        pltpu.VMEM((768, 2048), BF16),
        pltpu.VMEM((384, 1536), BF16),
        pltpu.VMEM((PIECE, 384), F32),
        pltpu.SMEM((1, 6), jnp.int32),
        pltpu.SemaphoreType.DMA((len(CHUNKS), N_SEMS)),
        pltpu.SemaphoreType.DMA((8,)),
        pltpu.SemaphoreType.REGULAR((3,)),
    ]
    hbm = pl.BlockSpec(memory_space=pl.ANY)
    vmem = pl.BlockSpec(memory_space=pltpu.VMEM)
    n, w = len(CHUNKS), CHUNKS[0][1]
    parts = pl.pallas_call(
        kernel,
        out_shape=(
            pltpu.VMEM((n, 256, w), F32),
            pltpu.VMEM((n, PIECE, w), F32),
        ),
        in_specs=[hbm] * 6,
        out_specs=(vmem, vmem),
        scratch_shapes=scratch,
        compiler_params=pltpu.CompilerParams(
            collective_id=0, has_side_effects=True, vmem_limit_bytes=60 * 2**20
        ),
        name="solve",
    )(*args)
    return pl.pallas_call(
        join,
        out_shape=(
            jax.ShapeDtypeStruct((256, 384), F32),
            jax.ShapeDtypeStruct((PIECE, 384), F32),
        ),
        in_specs=[vmem, vmem],
        out_specs=(vmem, vmem),
        name="join",
    )(*[pltpu.with_memory_space_constraint(part, pltpu.VMEM) for part in parts])


def solution(mesh):
    in_specs = (
        P(("front", "row"), None),
        P("row", None),
        P(("front", "row"), None),
        P(("front", "row"), None),
        P("front", "row"),
        P("front", "row"),
    )
    out_specs = (P(("front", "row"), None), P(("front", "row"), None))
    return jax.shard_map(
        per_device, mesh=mesh, in_specs=in_specs, out_specs=out_specs, check_vma=False
    )
```
